256 devices in a mesh: row: 8 (over z_hi, y), col: 32 (over z_lo, x, core).
Axes of the slice: x: 4, y: 4, z: 8 (z_hi: 2, z_lo: 4; z = z_hi * 4 + z_lo), core: 2. Of those that a mesh axis runs over, the one named last changes fastest.
Arguments:
- inputs: bfloat16 [1024, 9216], P('col', 'row'), may hold values from -6 to 6
- out_grad: bfloat16 [1024, 9216], P('col', 'row'), may hold values from -6 to 6
- preact: bfloat16 [1024, 36864], P('row', 'col'), may hold values from -6 to 6
- first_weight: bfloat16 [9216, 36864], P('row', 'col'), may hold values from -0.0625 to 0.0625
- second_weight: bfloat16 [36864, 9216], P('col', 'row'), may hold values from -0.03125 to 0.03125
Outputs:
- grad_inputs: float32 [1024, 9216], P('col', 'row')
- grad_first: bfloat16 [9216, 36864], P('row', 'col')
- grad_second: bfloat16 [36864, 9216], P('col', 'row')
The draws below stay inside these ranges and needn't reach their ends.
All inputs are finite; a program needn't handle non-finite values.
Results may differ from the reference program's by a relative error of at most 0.005.
Values may be sent and summed in bfloat16 or wider, within the bound.
No kernel may reach another device: no remote copies, remote signals or barrier semaphores. Data moves between devices by JAX's collectives and lax.ppermute only.
A program may use at most 64 MiB of HBM per device.

```python
import math
import jax
import jax.numpy as jnp
from jax import lax

D = 9216
FF = 36864
TOKENS = 1024


def block_levels(stream_key, shape, pieces, least, high):
    def one(dim, parts):
        heights = jax.random.uniform(jax.random.fold_in(jax.random.fold_in(stream_key, 6), dim), (parts,), jnp.float32, least / len(pieces), high / len(pieces))
        return jnp.repeat(jnp.exp(heights), shape[dim] // parts).reshape((-1,) + (1,) * (len(shape) - dim - 1))

    factor_of = one(*pieces[0])
    for cut in pieces[1:]:
        factor_of = factor_of * one(*cut)
    return factor_of


def normal_values(key, shape, width, reach, pieces=(), kind=jnp.bfloat16):
    values = jax.random.normal(key, shape, jnp.float32) * width
    if len(pieces) > 0:
        values = block_levels(key, shape, pieces, -0.22, 0.18) * values
    return jnp.clip(values, min=-reach, max=reach).astype(kind)


def setup_inputs(seed: int = 0) -> dict:
    keys = jax.random.split(jax.random.key(seed), 6)
    return {
        "inputs": normal_values(keys[0], (TOKENS, D), 1.0, 6.0, ((0, 32), (1, 8))),
        "out_grad": normal_values(keys[1], (TOKENS, D), 1.0, 6.0, ((0, 32), (1, 8))),
        "preact": normal_values(keys[2], (TOKENS, FF), 1.0, 6.0, ((0, 8), (1, 32))),
        "first_weight": normal_values(keys[3], (D, FF), D ** -0.5, 0.0625, ((0, 8), (1, 32))),
        "second_weight": normal_values(keys[4], (FF, D), FF ** -0.5, 0.03125, ((0, 32), (1, 8))),
    }


INV_ROOT_TWO = 0.7071067811865476
INV_ROOT_TWO_PI = 0.3989422804014327

def gelu_value(values):
    return 0.5 * values * (1.0 + lax.erf(values * INV_ROOT_TWO))

def gelu_slope(values):
    normal_cdf = 0.5 * (1.0 + lax.erf(values * INV_ROOT_TWO))
    density = jnp.exp(-0.5 * values * values) * INV_ROOT_TWO_PI
    return normal_cdf + values * density

def reference(inputs, out_grad, preact, first_weight, second_weight):
    factor = 1.0 / math.sqrt(TOKENS)
    hidden_pre = preact.astype(jnp.float32)
    activated = gelu_value(hidden_pre).astype(jnp.bfloat16)
    slopes = gelu_slope(hidden_pre)
    blocks = math.gcd(FF, 8)
    block_cols = FF // blocks

    def step(grad_total, block_id):
        offset = (block_id * block_cols).astype(jnp.int32)
        first_part = lax.dynamic_slice_in_dim(first_weight, offset, block_cols, 1)
        second_part = lax.dynamic_slice_in_dim(second_weight, offset, block_cols, 0)
        grad_act = lax.dot_general(out_grad, second_part, (((1,), (1,)), ((), ())), preferred_element_type=jnp.float32)
        slope_part = lax.dynamic_slice_in_dim(slopes, offset, block_cols, 1)
        grad_pre = (grad_act * slope_part).astype(jnp.bfloat16)
        act_part = lax.dynamic_slice_in_dim(activated, offset, block_cols, 1)
        first_part_grad = (lax.dot_general(inputs, grad_pre, (((0,), (0,)), ((), ())), preferred_element_type=jnp.float32) * factor).astype(jnp.bfloat16)
        second_part_grad = (lax.dot_general(act_part, out_grad, (((0,), (0,)), ((), ())), preferred_element_type=jnp.float32) * factor).astype(jnp.bfloat16)
        grad_total = grad_total + lax.dot_general(grad_pre, first_part, (((1,), (1,)), ((), ())), preferred_element_type=jnp.float32)
        return (grad_total, (first_part_grad, second_part_grad))
    grad_total, (first_parts, second_parts) = lax.scan(step, jnp.zeros((TOKENS, D), jnp.float32), jnp.arange(blocks, dtype=jnp.int32))
    grad_first = jnp.transpose(first_parts, (1, 0, 2)).reshape(D, FF)
    grad_second = second_parts.reshape(FF, D)
    return (grad_total, grad_first, grad_second)
```

```python
import functools
import math

import jax
import jax.numpy as jnp
from jax import lax
from jax.experimental import pallas as pl
from jax.experimental.pallas import tpu as pltpu
from jax.sharding import Mesh
from jax.sharding import PartitionSpec as P

INV_ROOT_TWO = 0.7071067811865476
INV_ROOT_TWO_PI = 0.3989422804014327
BF16 = jnp.bfloat16
F32 = jnp.float32


def gelu_value(values):
    return 0.5 * values * (1.0 + lax.erf(values * INV_ROOT_TWO))


def gelu_slope(values):
    normal_cdf = 0.5 * (1.0 + lax.erf(values * INV_ROOT_TWO))
    density = jnp.exp(-0.5 * values * values) * INV_ROOT_TWO_PI
    return normal_cdf + values * density


def contract_rows(left, right):
    return lax.dot_general(
        left, right, (((0,), (0,)), ((), ())), preferred_element_type=F32
    )


def contract_cols(left, right):
    return lax.dot_general(
        left, right, (((1,), (1,)), ((), ())), preferred_element_type=F32
    )


def shift(value, axis, step):
    size = lax.axis_size(axis)
    return lax.ppermute(value, axis, [(i, (i + step) % size) for i in range(size)])


def swap(value, axis):
    return lax.ppermute(value, axis, [(0, 1), (1, 0)])


def col_place_kernel(where, *refs):
    out = refs[-1]
    zl, x, c = where[0], where[1], where[2]
    for kc in range(2):
        for kx in range(4):
            for kz in range(4):
                out[
                    lax.rem(zl + 4 - kz, 4),
                    lax.rem(x + 4 - kx, 4),
                    lax.rem(c + kc, 2),
                ] = refs[kc * 4 + kx][kz]


def col_place(pieces):
    width = pieces[0].shape[-1]
    where = jnp.stack([lax.axis_index(a) for a in ("zl", "x", "c")]).astype(jnp.int32)
    rows = pieces[0].shape[1]
    whole = pl.pallas_call(
        col_place_kernel,
        out_shape=jax.ShapeDtypeStruct((4, 4, 2, rows, width), pieces[0].dtype),
        in_specs=[pl.BlockSpec(memory_space=pltpu.SMEM)]
        + [pl.BlockSpec(memory_space=pltpu.VMEM)] * 8,
        out_specs=pl.BlockSpec(memory_space=pltpu.VMEM),
        cost_estimate=pl.CostEstimate(
            flops=0, bytes_accessed=8 * 2 * pieces[0].size * 2, transcendentals=0
        ),
    )(where, *pieces)
    return whole.reshape(32 * rows, width)


def row_place_kernel(where, *refs):
    out = refs[-1]
    y = where[0]
    for ky in range(4):
        out[lax.rem(y + 4 - ky, 4)] = refs[ky][...]


def row_place(pieces):
    rows, width = pieces[0].shape
    where = lax.axis_index("y").astype(jnp.int32).reshape(1)
    whole = pl.pallas_call(
        row_place_kernel,
        out_shape=jax.ShapeDtypeStruct((4, rows, width), pieces[0].dtype),
        in_specs=[pl.BlockSpec(memory_space=pltpu.SMEM)]
        + [pl.BlockSpec(memory_space=pltpu.VMEM)] * 4,
        out_specs=pl.BlockSpec(memory_space=pltpu.VMEM),
        cost_estimate=pl.CostEstimate(
            flops=0, bytes_accessed=4 * 2 * pieces[0].size * 2, transcendentals=0
        ),
    )(where, *pieces)
    return whole.reshape(4 * rows, width)


def col_gather(own):
    line = jnp.stack([own] + [shift(own, "zl", k) for k in (1, 2, 3)])
    plane = [line] + [shift(line, "x", k) for k in (1, 2, 3)]
    return col_place(plane + [swap(p, "c") for p in plane])


def on_device(inputs, out_grad, preact, first_weight, second_weight):
    zh = lax.axis_index("zh")
    y = lax.axis_index("y")
    zl = lax.axis_index("zl")
    x = lax.axis_index("x")
    c = lax.axis_index("c")
    token_rows, width = preact.shape
    half = 4 * token_rows
    factor = 1.0 / math.sqrt(8 * token_rows)

    grad_whole = col_gather(out_grad)

    pre_far = swap(preact, "zh")
    pre_near = [preact] + [shift(preact, "y", k) for k in (1, 2, 3)]
    pre_far = [pre_far] + [shift(pre_far, "y", k) for k in (1, 2, 3)]
    pre_near, pre_far = row_place(pre_near), row_place(pre_far)

    def plane_sum(plane):
        rows = lax.dynamic_slice_in_dim(grad_whole, plane * half, half, 0)
        part = contract_cols(rows, second_weight).reshape(4, token_rows, width)
        total = lax.dynamic_index_in_dim(part, y, 0, keepdims=False)
        for k in (1, 2, 3):
            away = lax.dynamic_index_in_dim(part, (y + k) % 4, 0, keepdims=False)
            total = total + shift(away.astype(BF16), "y", k).astype(F32)
        return total

    from_far = swap(plane_sum(1 - zh).astype(BF16), "zh")
    grad_act = plane_sum(zh) + from_far.astype(F32)
    grad_own = (grad_act * gelu_slope(preact.astype(F32))).astype(BF16)

    gp_far = swap(grad_own, "zh")
    gp_near = row_place([grad_own] + [shift(grad_own, "y", k) for k in (1, 2, 3)])
    gp_far = row_place([gp_far] + [shift(gp_far, "y", k) for k in (1, 2, 3)])

    def plane_inputs(rows):
        split = rows.reshape(2, 4, 2, token_rows // 4, width)
        away = lax.dynamic_index_in_dim(split, 1 - c, 2, keepdims=False)
        keep = lax.dynamic_index_in_dim(split, c, 2, keepdims=False)
        away = contract_cols(away.reshape(-1, width), first_weight).astype(BF16)
        got = swap(away, "c")
        both = contract_cols(keep.reshape(-1, width), first_weight) + got.astype(F32)
        both = both.reshape(2, 4, token_rows // 4, width)
        total = lax.dynamic_index_in_dim(both, x, 1, keepdims=False)
        for k in (1, 2, 3):
            send = lax.dynamic_index_in_dim(both, (x + k) % 4, 1, keepdims=False)
            total = total + shift(send.astype(BF16), "x", k).astype(F32)
        return total

    near = plane_inputs(gp_near)
    far = plane_inputs(gp_far)
    order = zh == 0
    lines = jnp.concatenate([jnp.where(order, near, far), jnp.where(order, far, near)])
    grad_inputs = lax.dynamic_index_in_dim(lines, zl, 0, keepdims=False)
    for k in (1, 2, 3):
        send = lax.dynamic_index_in_dim(lines, (zl + k) % 4, 0, keepdims=False)
        grad_inputs = grad_inputs + shift(send.astype(BF16), "zl", k).astype(F32)

    def in_order(near, far):
        return jnp.concatenate([jnp.where(order, near, far), jnp.where(order, far, near)])

    activated = gelu_value(in_order(pre_near, pre_far).astype(F32)).astype(BF16)
    grad_second = (contract_rows(activated, grad_whole) * factor).astype(BF16)
    input_whole = col_gather(inputs)
    grad_pre = in_order(gp_near, gp_far)
    grad_first = (contract_rows(input_whole, grad_pre) * factor).astype(BF16)
    return (grad_inputs, grad_first, grad_second)


def solution(mesh):
    fine = Mesh(mesh.devices.reshape(2, 4, 4, 4, 2), ("zh", "y", "zl", "x", "c"))
    row, col = ("zh", "y"), ("zl", "x", "c")
    return jax.shard_map(
        on_device,
        mesh=fine,
        in_specs=(P(col, row), P(col, row), P(row, col), P(row, col), P(col, row)),
        out_specs=(P(col, row), P(row, col), P(col, row)),
        check_vma=False,
    )
```

```python
import math

import jax
import jax.numpy as jnp
from jax import lax
from jax.experimental import pallas as pl
from jax.experimental.pallas import tpu as pltpu
from jax.sharding import Mesh
from jax.sharding import PartitionSpec as P


INV_ROOT_TWO = 0.7071067811865476
INV_ROOT_TWO_PI = 0.3989422804014327
BF16 = jnp.bfloat16
F32 = jnp.float32


def gelu_value(values):
    return 0.5 * values * (1.0 + lax.erf(values * INV_ROOT_TWO))


def gelu_slope(values):
    normal_cdf = 0.5 * (1.0 + lax.erf(values * INV_ROOT_TWO))
    density = jnp.exp(-0.5 * values * values) * INV_ROOT_TWO_PI
    return normal_cdf + values * density


def contract_rows(left, right):
    return lax.dot_general(
        left, right, (((0,), (0,)), ((), ())), preferred_element_type=F32
    )


def contract_cols(left, right):
    return lax.dot_general(
        left, right, (((1,), (1,)), ((), ())), preferred_element_type=F32
    )


def shift(value, axis, step):
    size = lax.axis_size(axis)
    return lax.ppermute(value, axis, [(i, (i + step) % size) for i in range(size)])


def swap(value, axis):
    return lax.ppermute(value, axis, [(0, 1), (1, 0)])


def col_place_kernel(where, *refs):
    out = refs[-1]
    zh, y, zl, x, c = (where[i] for i in range(5))
    for kz in range(4):
        for kx in range(4):
            az = lax.rem(zl + 4 - kz, 4)
            ax = lax.rem(x + 4 - kx, 4)
            far = lax.rem(lax.div(az, 2) + zh, 2)
            ay = lax.rem(az, 2) * 2 + lax.div(ax, 2)
            step = lax.rem(ay + 4 - y, 4)
            for kc in range(2):
                out[far, step, lax.rem(ax, 2), lax.rem(c + kc, 2)] = refs[kc * 4 + kx][kz]


def col_place(where, pieces):
    rows, width = pieces[0].shape[1:]
    whole = pl.pallas_call(
        col_place_kernel,
        out_shape=jax.ShapeDtypeStruct((2, 4, 2, 2, rows, width), pieces[0].dtype),
        in_specs=[pl.BlockSpec(memory_space=pltpu.SMEM)]
        + [pl.BlockSpec(memory_space=pltpu.VMEM)] * 8,
        out_specs=pl.BlockSpec(memory_space=pltpu.VMEM),
        cost_estimate=pl.CostEstimate(
            flops=0, bytes_accessed=8 * 2 * pieces[0].size * 2, transcendentals=0
        ),
    )(where, *pieces)
    return whole.reshape(2, 16 * rows, width)


def spread(value, axis):
    got = {k: shift(value, axis, k) for k in (1, 2, 3)}
    return [value, got[3], got[2], got[1]]


def col_gather(where, own):
    line = jnp.stack([own] + [shift(own, "zl", k) for k in (1, 2, 3)])
    plane = [line] + [shift(line, "x", k) for k in (1, 2, 3)]
    other = []
    for piece in plane:
        other.append(swap(piece, "c"))
    return col_place(where, plane + other)


def compute(inputs, out_grad, preact, first_weight, second_weight):
    where = jnp.stack(
        [lax.axis_index(a) for a in ("zh", "y", "zl", "x", "c")]
    ).astype(jnp.int32)
    zh, y, zl, x, c = (where[i] for i in range(5))
    token_rows, width = preact.shape
    block = token_rows // 4
    factor = 1.0 / math.sqrt(8 * token_rows)

    grad_near, grad_far = jnp.split(col_gather(where, out_grad), 2)
    grad_near, grad_far = grad_near[0], grad_far[0]

    pre = spread(preact, "y")
    pre_far = swap(preact, "zh")
    pre += spread(pre_far, "y")

    def plane_sum(rows):
        part = contract_cols(rows, second_weight).reshape(4, token_rows, width)
        got = [shift(part[k].astype(BF16), "y", k) for k in (1, 2, 3)]
        return part[0] + sum(g.astype(F32) for g in got)

    far_sum = plane_sum(grad_far).astype(BF16)
    near_sum = plane_sum(grad_near)
    from_far = swap(far_sum, "zh")
    grad_act = near_sum + from_far.astype(F32)
    grad_own = (grad_act * gelu_slope(preact.astype(F32))).astype(BF16)

    near = spread(grad_own, "y")
    own_far = swap(grad_own, "zh")
    far = spread(own_far, "y")

    def plane_inputs(pieces):
        def rows(core):
            parts = [
                lax.dynamic_index_in_dim(
                    p.reshape(2, 2, block, width), core, 1, keepdims=False
                )
                for p in pieces
            ]
            return jnp.stack(parts).reshape(-1, width)

        away = contract_cols(rows(1 - c), first_weight).astype(BF16)
        got = swap(away, "c")
        both = contract_cols(rows(c), first_weight) + got.astype(F32)
        both = both.reshape(4, 2, block, width)

        def to(ax):
            lines = []
            for zlow in range(2):
                step = lax.rem(zlow * 2 + lax.div(ax, 2) + 4 - y, 4)
                start = (step, lax.rem(ax, 2), 0, 0)
                lines.append(lax.dynamic_slice(both, start, (1, 1, block, width))[0])
            return jnp.concatenate(lines)

        total = to(x)
        sends = [to(lax.rem(x + k, 4)).astype(BF16) for k in (1, 2, 3)]
        got = [shift(s, "x", k) for k, s in zip((1, 2, 3), sends)]
        return total + sum(g.astype(F32) for g in got)

    near_lines = plane_inputs(near)
    far_lines = plane_inputs(far)
    ahead = zh == 0
    lines = jnp.concatenate(
        [jnp.where(ahead, near_lines, far_lines), jnp.where(ahead, far_lines, near_lines)]
    )
    grad_inputs = lax.dynamic_index_in_dim(lines, zl, 0, keepdims=False)
    sends = [
        lax.dynamic_index_in_dim(lines, lax.rem(zl + k, 4), 0, keepdims=False).astype(BF16)
        for k in (1, 2, 3)
    ]
    got = [shift(s, "zl", k) for k, s in zip((1, 2, 3), sends)]
    grad_inputs = grad_inputs + sum(g.astype(F32) for g in got)

    grad_rows = jnp.concatenate([grad_near, grad_far])
    activated = gelu_value(jnp.concatenate(pre).astype(F32)).astype(BF16)
    grad_second = (contract_rows(activated, grad_rows) * factor).astype(BF16)
    input_rows = col_gather(where, inputs).reshape(8 * token_rows, width)
    grad_pre = jnp.concatenate(near + far)
    grad_first = (contract_rows(input_rows, grad_pre) * factor).astype(BF16)
    return (grad_inputs, grad_first, grad_second)


def solution(mesh):
    fine = Mesh(mesh.devices.reshape(2, 4, 4, 4, 2), ("zh", "y", "zl", "x", "c"))
    row, col = ("zh", "y"), ("zl", "x", "c")
    return jax.shard_map(
        compute,
        mesh=fine,
        in_specs=(P(col, row), P(col, row), P(row, col), P(row, col), P(col, row)),
        out_specs=(P(col, row), P(row, col), P(col, row)),
        check_vma=False,
    )
```

```python
import math

import jax
import jax.numpy as jnp
from jax import lax
from jax.experimental import pallas as pl
from jax.experimental.pallas import tpu as pltpu
from jax.sharding import Mesh
from jax.sharding import PartitionSpec as P


INV_ROOT_TWO = 0.7071067811865476
INV_ROOT_TWO_PI = 0.3989422804014327
BF16 = jnp.bfloat16
F32 = jnp.float32


def gelu_value(values):
    return 0.5 * values * (1.0 + lax.erf(values * INV_ROOT_TWO))


def gelu_slope(values):
    normal_cdf = 0.5 * (1.0 + lax.erf(values * INV_ROOT_TWO))
    density = jnp.exp(-0.5 * values * values) * INV_ROOT_TWO_PI
    return normal_cdf + values * density


def shift(value, axis, step):
    size = lax.axis_size(axis)
    return lax.ppermute(value, axis, [(i, (i + step) % size) for i in range(size)])


def swap(value, axis):
    return lax.ppermute(value, axis, [(0, 1), (1, 0)])


VMEM = pl.BlockSpec(memory_space=pltpu.VMEM)
SMEM = pl.BlockSpec(memory_space=pltpu.SMEM)


def cost(flops, moved):
    return pl.CostEstimate(flops=flops, bytes_accessed=moved, transcendentals=0)


def times(left, right):
    return lax.dot_general(left, right, (((1,), (1,)), ((), ())), preferred_element_type=F32)


def col_place_kernel(where, *refs):
    out = refs[-1]
    zh, y, zl, x = (where[i] for i in range(4))
    for kz in range(4):
        for kx in range(4):
            az = lax.rem(zl + 4 - kz, 4)
            ax = lax.rem(x + 4 - kx, 4)
            far = lax.rem(lax.div(az, 2) + zh, 2)
            ay = lax.rem(az, 2) * 2 + lax.div(ax, 2)
            out[far, lax.rem(ay + 4 - y, 4), lax.rem(ax, 2)] = refs[kx][kz]


def col_place(where, pieces):
    rows, width = pieces[0].shape[1:]
    return pl.pallas_call(
        col_place_kernel,
        out_shape=jax.ShapeDtypeStruct((2, 4, 2, rows, width), BF16),
        in_specs=[SMEM] + [VMEM] * 4,
        out_specs=VMEM,
        cost_estimate=cost(0, 16 * pieces[0].size),
    )(where, *pieces)


def shifts(value, axis):
    return [value] + [shift(value, axis, k) for k in (1, 2, 3)]


def spread(value):
    own, one, two, three = shifts(value, "y")
    return [own, three, two, one]


def col_gather(where, own):
    line = jnp.stack(shifts(own, "zl"))
    half = col_place(where, shifts(line, "x"))
    return half, swap(half, "c")


def own_act_kernel(half, weight, part, first):
    for far in range(2):
        rows = half[far].reshape(-1, half.shape[-1])
        got = times(rows, weight[...]).reshape(part.shape[1:])
        part[far] = got.astype(BF16)
        first[far] = got[0]


def own_act(half, weight):
    width = weight.shape[0]
    rows = half.shape[2] * half.shape[3]
    return pl.pallas_call(
        own_act_kernel,
        out_shape=(
            jax.ShapeDtypeStruct((2, 4, rows, width), BF16),
            jax.ShapeDtypeStruct((2, rows, width), F32),
        ),
        in_specs=[VMEM] * 2,
        out_specs=(VMEM,) * 2,
        cost_estimate=cost(2 * half.size * width, 4 * half.size + 2 * weight.size),
    )(half, weight)


def other_act_kernel(far, half, weight, part, first, keep, one, two, three):
    rows = part.shape[2]
    got = times(half[far].reshape(-1, half.shape[-1]), weight[...])
    keep[:rows] = first[far]
    keep[rows:] = got[:rows]
    for k, send in ((1, one), (2, two), (3, three)):
        send[:rows] = part[far, k]
        send[rows:] = got[k * rows : (k + 1) * rows].astype(BF16)


def other_act(far, half, weight, part, first):
    width = weight.shape[0]
    rows = 2 * part.shape[2]
    return pl.pallas_call(
        lambda *refs: other_act_kernel(far, *refs),
        out_shape=(jax.ShapeDtypeStruct((rows, width), F32),)
        + (jax.ShapeDtypeStruct((rows, width), BF16),) * 3,
        in_specs=[VMEM] * 4,
        out_specs=(VMEM,) * 4,
        cost_estimate=cost(half.size * width, 6 * half.size + 2 * weight.size),
    )(half, weight, part, first)


def token_kernel(where, p0, p1, p2, p3, weight, away, keep, rows):
    y, x = where[1], where[3]
    block = rows.shape[3]
    for j, piece in enumerate((p0, p1, p2, p3)):
        ay = lax.rem(y + j, 4)
        for low in range(2):
            ax = lax.rem(ay, 2) * 2 + low
            kx = lax.rem(ax + 4 - x, 4)
            for core in range(2):
                start = (core * 2 + low) * block
                rows[core, kx, lax.div(ay, 2)] = piece[start : start + block]
    whole = (-1, rows.shape[-1])
    away[...] = times(rows[1].reshape(whole), weight[...]).astype(BF16).reshape(away.shape)
    keep[...] = times(rows[0].reshape(whole), weight[...]).reshape(keep.shape)


def token_products(where, pieces, weight):
    token_rows, width = pieces[0].shape
    shape = (4, 2, token_rows // 4, weight.shape[0])
    return pl.pallas_call(
        token_kernel,
        out_shape=(jax.ShapeDtypeStruct(shape, BF16), jax.ShapeDtypeStruct(shape, F32)),
        in_specs=[SMEM] + [VMEM] * 5,
        out_specs=(VMEM,) * 2,
        scratch_shapes=[pltpu.VMEM((2, 4, 2, token_rows // 4, width), BF16)],
        cost_estimate=cost(
            8 * token_rows * width * width, 2 * weight.size + 20 * token_rows * width
        ),
    )(where, *pieces, weight)


def line_kernel(where, *refs):
    zh, zl = where[0], where[2]
    near, far, outs, sums = refs[:4], refs[4:8], refs[8:12], refs[12]
    for plane, (kept, one, two, three) in enumerate((near, far)):
        for low in range(2):
            sums[plane * 2 + low] = (
                kept[low]
                + one[low].astype(F32)
                + two[low].astype(F32)
                + three[low].astype(F32)
            )
    for k, out in enumerate(outs):
        az = lax.rem(zl + k, 4)
        plane = lax.rem(lax.div(az, 2) + zh, 2)
        out[...] = sums[plane * 2 + lax.rem(az, 2)].astype(out.dtype)


def line_sums(where, near, far):
    _, block, width = near[0].shape
    return pl.pallas_call(
        line_kernel,
        out_shape=(jax.ShapeDtypeStruct((block, width), F32),)
        + (jax.ShapeDtypeStruct((block, width), BF16),) * 3,
        in_specs=[SMEM] + [VMEM] * 8,
        out_specs=(VMEM,) * 4,
        scratch_shapes=[pltpu.VMEM((4, block, width), F32)],
        cost_estimate=cost(0, 40 * block * width),
    )(where, *near, *far)


CHUNK = 384


def outer(left, own, other, low, factor):
    columns = pl.ds(low, CHUNK)
    half = left.shape[0] // 2
    dims = (((0,), (0,)), ((), ()))
    total = lax.dot_general(left[:half, columns], own, dims, preferred_element_type=F32)
    total += lax.dot_general(left[half:, columns], other, dims, preferred_element_type=F32)
    return (total * factor).astype(BF16)


def second_kernel(factor, *refs):
    pieces, (own, other, out, act) = refs[:8], refs[8:]
    rows = pieces[0].shape[0] // 2
    width = own.shape[-1]

    @pl.when(pl.program_id(0) == 0)
    def _():
        for i, piece in enumerate(pieces):
            for core in range(2):
                values = piece[core * rows : (core + 1) * rows].astype(F32)
                start = (core * 8 + i) * rows
                act[start : start + rows] = gelu_value(values).astype(BF16)

    low = pl.multiple_of(pl.program_id(0) * CHUNK, CHUNK)
    out[...] = outer(
        act, own[...].reshape(-1, width), other[...].reshape(-1, width), low, factor
    )


def first_kernel(factor, *refs):
    pieces, (own, other, out, left, right) = refs[:8], refs[8:]
    rows = pieces[0].shape[0] // 2
    width = own.shape[-1]
    half = 8 * rows

    @pl.when(pl.program_id(0) == 0)
    def _():
        for i, piece in enumerate(pieces):
            for core in range(2):
                start = (core * 8 + i) * rows
                right[start : start + rows] = piece[core * rows : (core + 1) * rows]
        left[:half] = own[...].reshape(-1, width)
        left[half:] = other[...].reshape(-1, width)

    low = pl.multiple_of(pl.program_id(0) * CHUNK, CHUNK)
    out[...] = outer(left, right[:half], right[half:], low, factor)


def token_outer(kernel, pieces, halves, factor, scratches):
    token_rows, width = pieces[0].shape
    tokens = 8 * token_rows
    left = width if scratches == 1 else halves[0].shape[-1]
    right = halves[0].shape[-1] if scratches == 1 else width

    def whole(a):
        return pl.BlockSpec(a.shape, lambda i, n=a.ndim: (0,) * n)

    return pl.pallas_call(
        lambda *refs: kernel(factor, *refs),
        out_shape=jax.ShapeDtypeStruct((left, right), BF16),
        grid=(left // CHUNK,),
        in_specs=[whole(a) for a in (*pieces, *halves)],
        out_specs=pl.BlockSpec((CHUNK, right), lambda i: (i, 0)),
        scratch_shapes=[pltpu.VMEM((tokens, width), BF16)] * scratches,
        cost_estimate=cost(
            2 * tokens * left * right, 4 * tokens * width + 2 * left * right
        ),
    )(*pieces, *halves)


def compute(inputs, out_grad, preact, first_weight, second_weight):
    where = jnp.stack(
        [lax.axis_index(a) for a in ("zh", "y", "zl", "x", "c")]
    ).astype(jnp.int32)
    c = where[4]
    token_rows, width = preact.shape
    block = token_rows // 4
    factor = 1.0 / math.sqrt(8 * token_rows)

    split = preact.reshape(2, 2, block, width)
    preact = jnp.stack(
        [
            jnp.where(c == 0, split[:, 0], split[:, 1]),
            jnp.where(c == 0, split[:, 1], split[:, 0]),
        ]
    ).reshape(token_rows, width)

    grad_half, grad_other = col_gather(where, out_grad)
    pre = spread(preact)
    pre_far = swap(preact, "zh")
    pre += spread(pre_far)

    part, first = own_act(grad_half, second_weight)

    def plane_sum(far):
        keep, *sends = other_act(far, grad_other, second_weight, part, first)
        got = [shift(s, "y", k) for k, s in zip((1, 2, 3), sends)]
        return keep + sum(g.astype(F32) for g in got)

    far_sum = plane_sum(1).astype(BF16)
    near_sum = plane_sum(0)
    from_far = swap(far_sum, "zh")
    grad_act = near_sum + from_far.astype(F32)
    grad_own = (grad_act * gelu_slope(preact.astype(F32))).astype(BF16)

    near = spread(grad_own)
    own_far = swap(grad_own, "zh")
    far = spread(own_far)

    def plane_inputs(pieces):
        away, keep = token_products(where, pieces, first_weight)
        got = swap(away, "c")
        both = keep + got.astype(F32)
        sends = [both[k].astype(BF16) for k in (1, 2, 3)]
        return [both[0]] + [shift(s, "x", k) for k, s in zip((1, 2, 3), sends)]

    near_lines = plane_inputs(near)
    far_lines = plane_inputs(far)
    grad_inputs, *sends = line_sums(where, near_lines, far_lines)
    got = [shift(s, "zl", k) for k, s in zip((1, 2, 3), sends)]
    grad_inputs = grad_inputs + sum(g.astype(F32) for g in got)

    halves = col_gather(where, inputs)
    grad_first = token_outer(first_kernel, near + far, halves, factor, 2)
    grad_second = token_outer(second_kernel, pre, (grad_half, grad_other), factor, 1)
    return (grad_inputs, grad_first, grad_second)


def solution(mesh):
    fine = Mesh(mesh.devices.reshape(2, 4, 4, 4, 2), ("zh", "y", "zl", "x", "c"))
    row, col = ("zh", "y"), ("zl", "x", "c")
    return jax.shard_map(
        compute,
        mesh=fine,
        in_specs=(P(col, row), P(col, row), P(row, col), P(row, col), P(col, row)),
        out_specs=(P(col, row), P(row, col), P(col, row)),
        check_vma=False,
    )
```

```python
import math

import jax
import jax.numpy as jnp
from jax import lax
from jax.experimental import pallas as pl
from jax.experimental.pallas import tpu as pltpu
from jax.sharding import Mesh
from jax.sharding import PartitionSpec as P


INV_ROOT_TWO = 0.7071067811865476
INV_ROOT_TWO_PI = 0.3989422804014327
BF16 = jnp.bfloat16
F32 = jnp.float32


def gelu_value(values):
    return 0.5 * values * (1.0 + lax.erf(values * INV_ROOT_TWO))


def gelu_slope(values):
    normal_cdf = 0.5 * (1.0 + lax.erf(values * INV_ROOT_TWO))
    density = jnp.exp(-0.5 * values * values) * INV_ROOT_TWO_PI
    return normal_cdf + values * density


def shift(value, axis, step):
    size = lax.axis_size(axis)
    return lax.ppermute(value, axis, [(i, (i + step) % size) for i in range(size)])


def swap(value, axis):
    return lax.ppermute(value, axis, [(0, 1), (1, 0)])


VMEM = pl.BlockSpec(memory_space=pltpu.VMEM)
SMEM = pl.BlockSpec(memory_space=pltpu.SMEM)


def cost(flops, moved):
    return pl.CostEstimate(flops=flops, bytes_accessed=moved, transcendentals=0)


def call(kernel, outs, operands, scratch=(), where=None, flops=0, hbm_out=False):
    moved = sum(2 * o.size for o in operands)
    operands = [pltpu.with_memory_space_constraint(o, pltpu.VMEM) for o in operands]
    specs = [VMEM] * len(operands)
    if where is not None:
        operands, specs = [where] + operands, [SMEM] + specs
    space = pl.BlockSpec(memory_space=pl.ANY) if hbm_out else VMEM
    make = jax.ShapeDtypeStruct if hbm_out else pltpu.VMEM
    return pl.pallas_call(
        kernel,
        out_shape=tuple(make(shape, dtype) for shape, dtype in outs),
        in_specs=specs,
        out_specs=(space,) * len(outs),
        scratch_shapes=scratch,
        cost_estimate=cost(flops, moved),
        compiler_params=pltpu.CompilerParams(vmem_limit_bytes=GRANT),
    )(*operands)


GRANT = 12 * 1024 * 1024


def times(left, right):
    return lax.dot_general(left, right, (((1,), (1,)), ((), ())), preferred_element_type=F32)


def col_place_kernel(where, *refs):
    out = refs[-1]
    zh, y, zl, x = (where[i] for i in range(4))
    for kz in range(4):
        for kx in range(4):
            az = lax.rem(zl + 4 - kz, 4)
            ax = lax.rem(x + 4 - kx, 4)
            far = lax.rem(lax.div(az, 2) + zh, 2)
            ay = lax.rem(az, 2) * 2 + lax.div(ax, 2)
            out[far, lax.rem(ay + 4 - y, 4), lax.rem(ax, 2)] = refs[kx][kz]


def col_place(where, pieces):
    rows, width = pieces[0].shape[1:]
    return call(
        col_place_kernel, [((2, 4, 2, rows, width), BF16)], pieces, where=where
    )[0]


def shifts(value, axis):
    return [value] + [shift(value, axis, k) for k in (1, 2, 3)]


def spread(value):
    own, one, two, three = shifts(value, "y")
    return [own, three, two, one]


def col_gather(where, own):
    line = jnp.stack(shifts(own, "zl"))
    half = col_place(where, shifts(line, "x"))
    return half, swap(half, "c")


def own_act_kernel(half, weight, part, first):
    @pl.loop(0, 2)
    def _(far):
        rows = half[far].reshape(-1, half.shape[-1])
        got = times(rows, weight[...]).reshape(part.shape[1:])
        part[far] = got.astype(BF16)
        first[far] = got[0]


def own_act(half, weight):
    width = weight.shape[0]
    rows = half.shape[2] * half.shape[3]
    return call(
        own_act_kernel,
        [((2, 4, rows, width), BF16), ((2, rows, width), F32)],
        [half, weight],
        flops=2 * half.size * width,
    )


def other_act_kernel(far, half, weight, part, first, keep, one, two, three):
    rows = part.shape[2]
    got = times(half[far].reshape(-1, half.shape[-1]), weight[...])
    keep[:rows] = first[far]
    keep[rows:] = got[:rows]
    for k, send in ((1, one), (2, two), (3, three)):
        send[:rows] = part[far, k]
        send[rows:] = got[k * rows : (k + 1) * rows].astype(BF16)


def other_act(far, half, weight, part, first):
    width = weight.shape[0]
    rows = 2 * part.shape[2]
    return call(
        lambda *refs: other_act_kernel(far, *refs),
        [((rows, width), F32)] + [((rows, width), BF16)] * 3,
        [half, weight, part, first],
        flops=half.size * width,
    )


def token_kernel(where, p0, p1, p2, p3, weight, away, keep, rows):
    y, x = where[1], where[3]
    block = rows.shape[3]
    for j, piece in enumerate((p0, p1, p2, p3)):
        ay = lax.rem(y + j, 4)
        for low in range(2):
            ax = lax.rem(ay, 2) * 2 + low
            kx = lax.rem(ax + 4 - x, 4)
            for core in range(2):
                start = (core * 2 + low) * block
                rows[core, kx, lax.div(ay, 2)] = piece[start : start + block]

    @pl.loop(0, 2)
    def _(core):
        got = times(rows[core].reshape(-1, rows.shape[-1]), weight[...])

        @pl.when(core == 0)
        def _():
            keep[...] = got.reshape(keep.shape)

        @pl.when(core == 1)
        def _():
            away[...] = got.astype(BF16).reshape(away.shape)


def token_products(where, pieces, weight):
    token_rows, width = pieces[0].shape
    shape = (4, 2, token_rows // 4, weight.shape[0])
    return call(
        token_kernel,
        [(shape, BF16), (shape, F32)],
        [*pieces, weight],
        scratch=[pltpu.VMEM((2, 4, 2, token_rows // 4, width), BF16)],
        where=where,
        flops=8 * token_rows * width * width,
    )


def line_send_kernel(near, near_got, far, far_got, keep, one, two, three):
    for plane, (own, got) in enumerate(((near, near_got), (far, far_got))):
        for k, out in enumerate((keep, one, two, three)):
            out[plane] = (own[k] + got[k].astype(F32)).astype(out.dtype)


def line_sends(near, near_got, far, far_got):
    shape = (2, *near.shape[1:])
    return call(
        line_send_kernel,
        [(shape, F32)] + [(shape, BF16)] * 3,
        [near, near_got, far, far_got],
    )


def line_kernel(where, kept, one, two, three, *outs_sums):
    zh, zl = where[0], where[2]
    outs, sums = outs_sums[:4], outs_sums[4]
    sums[...] = (
        kept[...] + one[...].astype(F32) + two[...].astype(F32) + three[...].astype(F32)
    )
    for k, out in enumerate(outs):
        az = lax.rem(zl + k, 4)
        plane = lax.rem(lax.div(az, 2) + zh, 2)
        out[...] = sums[plane, lax.rem(az, 2)].astype(out.dtype)


def line_sums(where, lines):
    block, width = lines[0].shape[2:]
    return call(
        line_kernel,
        [((block, width), F32)] + [((block, width), BF16)] * 3,
        lines,
        scratch=[pltpu.VMEM((2, 2, block, width), F32)],
        where=where,
    )


CHUNK = 384


def outer(lefts, rights, out, stage, sem, factor):
    dims = (((0,), (0,)), ((), ()))

    def send(i):
        start = pl.multiple_of(i * CHUNK, CHUNK)
        return pltpu.make_async_copy(stage.at[i], out.at[pl.ds(start, CHUNK)], sem.at[i])

    @pl.loop(0, out.shape[0] // CHUNK)
    def _(i):
        columns = pl.ds(pl.multiple_of(i * CHUNK, CHUNK), CHUNK)
        total = sum(
            lax.dot_general(left(columns), right(), dims, preferred_element_type=F32)
            for left, right in zip(lefts, rights)
        )
        stage[i] = (total * factor).astype(BF16)
        send(i).start()

    for i in range(out.shape[0] // CHUNK):
        send(i).wait()


def second_kernel(factor, *refs):
    pieces, (own, other, out, act, stage, sem) = refs[:4], refs[4:]
    rows = pieces[0].shape[1] // 2
    width = own.shape[-1]
    for j, piece in enumerate(pieces):

        @pl.loop(0, 4)
        def _(i):
            far, core = lax.div(i, 2), lax.rem(i, 2)
            values = piece[far, pl.ds(core * rows, rows)].astype(F32)
            start = (core * 8 + far * 4 + j) * rows
            act[pl.ds(start, rows)] = gelu_value(values).astype(BF16)

    half = 8 * rows
    lefts = [lambda cols, n=n: act[n * half : (n + 1) * half, cols] for n in range(2)]
    rights = [lambda h=h: h[...].reshape(-1, width) for h in (own, other)]
    outer(lefts, rights, out, stage, sem, factor)


def first_kernel(factor, *refs):
    pieces, (own, other, out, right, stage, sem) = refs[:8], refs[8:]
    rows = pieces[0].shape[0] // 2
    half = 8 * rows
    for i, piece in enumerate(pieces):

        @pl.loop(0, 2)
        def _(core):
            right[pl.ds((core * 8 + i) * rows, rows)] = piece[pl.ds(core * rows, rows)]

    lefts = [
        lambda cols, h=h: h[:, :, :, :, cols].reshape(-1, CHUNK) for h in (own, other)
    ]
    rights = [lambda n=n: right[n * half : (n + 1) * half] for n in range(2)]
    outer(lefts, rights, out, stage, sem, factor)


def token_outer(kernel, pieces, halves, factor, swapped):
    width = pieces[0].shape[-1]
    tokens = sum(p.size for p in pieces) // width
    left, right = width, halves[0].shape[-1]
    if swapped:
        left, right = right, left
    return call(
        lambda *refs: kernel(factor, *refs),
        [((left, right), BF16)],
        [*pieces, *halves],
        scratch=[
            pltpu.VMEM((tokens, width), BF16),
            pltpu.VMEM((left // CHUNK, CHUNK, right), BF16),
            pltpu.SemaphoreType.DMA((left // CHUNK,)),
        ],
        flops=2 * tokens * left * right,
        hbm_out=True,
    )[0]


def compute(inputs, out_grad, preact, first_weight, second_weight):
    where = jnp.stack(
        [lax.axis_index(a) for a in ("zh", "y", "zl", "x", "c")]
    ).astype(jnp.int32)
    c = where[4]
    token_rows, width = preact.shape
    block = token_rows // 4
    factor = 1.0 / math.sqrt(8 * token_rows)

    split = preact.reshape(2, 2, block, width)
    preact = jnp.stack(
        [
            jnp.where(c == 0, split[:, 0], split[:, 1]),
            jnp.where(c == 0, split[:, 1], split[:, 0]),
        ]
    ).reshape(token_rows, width)

    grad_half, grad_other = col_gather(where, out_grad)
    pre_far = swap(preact, "zh")
    pre = spread(jnp.stack([preact, pre_far]))

    part, first = own_act(grad_half, second_weight)

    def plane_sum(far):
        keep, *sends = other_act(far, grad_other, second_weight, part, first)
        got = [shift(s, "y", k) for k, s in zip((1, 2, 3), sends)]
        return keep + sum(g.astype(F32) for g in got)

    far_sum = plane_sum(1).astype(BF16)
    near_sum = plane_sum(0)
    from_far = swap(far_sum, "zh")
    grad_act = near_sum + from_far.astype(F32)
    grad_own = (grad_act * gelu_slope(preact.astype(F32))).astype(BF16)

    near = spread(grad_own)
    own_far = swap(grad_own, "zh")
    far = spread(own_far)

    def plane_inputs(pieces):
        away, keep = token_products(where, pieces, first_weight)
        return keep, swap(away, "c")

    keep, *sends = line_sends(*plane_inputs(near), *plane_inputs(far))
    lines = [keep] + [shift(s, "x", k) for k, s in zip((1, 2, 3), sends)]
    grad_inputs, *sends = line_sums(where, lines)
    got = [shift(s, "zl", k) for k, s in zip((1, 2, 3), sends)]
    grad_inputs = grad_inputs + sum(g.astype(F32) for g in got)

    halves = col_gather(where, inputs)
    grad_first = token_outer(first_kernel, near + far, halves, factor, True)
    grad_second = token_outer(
        second_kernel, pre, (grad_half, grad_other), factor, False
    )
    return (grad_inputs, grad_first, grad_second)


def solution(mesh):
    fine = Mesh(mesh.devices.reshape(2, 4, 4, 4, 2), ("zh", "y", "zl", "x", "c"))
    row, col = ("zh", "y"), ("zl", "x", "c")
    return jax.shard_map(
        compute,
        mesh=fine,
        in_specs=(P(col, row), P(col, row), P(row, col), P(row, col), P(col, row)),
        out_specs=(P(col, row), P(row, col), P(col, row)),
        check_vma=False,
    )
```

```python
import math

import jax
import jax.numpy as jnp
from jax import lax
from jax.experimental import pallas as pl
from jax.experimental.pallas import tpu as pltpu
from jax.sharding import Mesh
from jax.sharding import PartitionSpec as P


INV_ROOT_TWO = 0.7071067811865476
INV_ROOT_TWO_PI = 0.3989422804014327
BF16 = jnp.bfloat16
F32 = jnp.float32


def gelu_value(values):
    return 0.5 * values * (1.0 + lax.erf(values * INV_ROOT_TWO))


def gelu_slope(values):
    normal_cdf = 0.5 * (1.0 + lax.erf(values * INV_ROOT_TWO))
    density = jnp.exp(-0.5 * values * values) * INV_ROOT_TWO_PI
    return normal_cdf + values * density


def shift(value, axis, step):
    size = lax.axis_size(axis)
    return lax.ppermute(value, axis, [(i, (i + step) % size) for i in range(size)])


def flip(value, axis, mask):
    size = lax.axis_size(axis)
    return lax.ppermute(value, axis, [(i, i ^ mask) for i in range(size)])


def swap(value, axis):
    return lax.ppermute(value, axis, [(0, 1), (1, 0)])


VMEM = pl.BlockSpec(memory_space=pltpu.VMEM)
SMEM = pl.BlockSpec(memory_space=pltpu.SMEM)


def cost(flops, moved):
    return pl.CostEstimate(flops=flops, bytes_accessed=moved, transcendentals=0)


def call(kernel, outs, operands, scratch=(), where=None, flops=0, hbm_out=False):
    moved = sum(2 * o.size for o in operands)
    operands = [pltpu.with_memory_space_constraint(o, pltpu.VMEM) for o in operands]
    specs = [VMEM] * len(operands)
    if where is not None:
        operands, specs = [where] + operands, [SMEM] + specs
    space = pl.BlockSpec(memory_space=pl.ANY) if hbm_out else VMEM
    make = jax.ShapeDtypeStruct if hbm_out else pltpu.VMEM
    return pl.pallas_call(
        kernel,
        out_shape=tuple(make(shape, dtype) for shape, dtype in outs),
        in_specs=specs,
        out_specs=(space,) * len(outs),
        scratch_shapes=scratch,
        cost_estimate=cost(flops, moved),
        compiler_params=pltpu.CompilerParams(vmem_limit_bytes=GRANT),
    )(*operands)


GRANT = 12 * 1024 * 1024


def times(left, right):
    return lax.dot_general(left, right, (((1,), (1,)), ((), ())), preferred_element_type=F32)


def place(where, out, az, ax, block):
    zh, y = where[0], where[1]
    far = lax.rem(lax.div(az, 2) + zh, 2)
    ay = lax.rem(az, 2) * 2 + lax.div(ax, 2)
    out[far, lax.rem(ay + 4 - y, 4), lax.rem(ax, 2)] = block


def shift_place_kernel(where, *refs):
    for kz in range(4):
        for kx in range(4):
            az = lax.rem(where[2] + 4 - kz, 4)
            ax = lax.rem(where[3] + 4 - kx, 4)
            place(where, refs[-1], az, ax, refs[kx][kz])


def flip_place_kernel(where, near, far, out):
    for kz in range(4):
        for kx in range(4):
            az = lax.bitwise_xor(where[2], kz)
            ax = lax.bitwise_xor(where[3], kx)
            place(where, out, az, ax, (near, far)[kx // 2][kx % 2, kz])


def col_place(kernel, where, pieces):
    rows, width = pieces[0].shape[-2:]
    return call(kernel, [((2, 4, 2, rows, width), BF16)], pieces, where=where)[0]


def shifts(value, axis):
    got = [value]
    for k in (1, 2, 3):
        got.append(shift(value, axis, k))
    return got


def spread(value):
    own, one, two, three = shifts(value, "y")
    return [own, three, two, one]


def gather_shifts(where, own):
    line = jnp.stack(shifts(own, "zl"))
    return col_place(shift_place_kernel, where, shifts(line, "x"))


def gather_flips(where, own):
    pair = jnp.stack([own, flip(own, "zl", 1)])
    line = jnp.concatenate([pair, flip(pair, "zl", 2)])
    lines = jnp.stack([line, flip(line, "x", 1)])
    rest = flip(lines, "x", 2)
    return col_place(flip_place_kernel, where, [lines, rest])


def own_act_kernel(half, weight, part, first):
    @pl.loop(0, 2)
    def _(far):
        rows = half[far].reshape(-1, half.shape[-1])
        got = times(rows, weight[...]).reshape(part.shape[1:])
        part[far] = got.astype(BF16)
        first[far] = got[0]


def own_act(half, weight):
    width = weight.shape[0]
    rows = half.shape[2] * half.shape[3]
    return call(
        own_act_kernel,
        [((2, 4, rows, width), BF16), ((2, rows, width), F32)],
        [half, weight],
        flops=2 * half.size * width,
    )


def other_act_kernel(far, half, weight, part, first, keep, one, two, three):
    rows = part.shape[2]
    got = times(half[far].reshape(-1, half.shape[-1]), weight[...])
    keep[:rows] = first[far]
    keep[rows:] = got[:rows]
    for k, send in ((1, one), (2, two), (3, three)):
        send[:rows] = part[far, k]
        send[rows:] = got[k * rows : (k + 1) * rows].astype(BF16)


def other_act(far, half, weight, part, first):
    width = weight.shape[0]
    rows = 2 * part.shape[2]
    return call(
        lambda *refs: other_act_kernel(far, *refs),
        [((rows, width), F32)] + [((rows, width), BF16)] * 3,
        [half, weight, part, first],
        flops=half.size * width,
    )


def token_kernel(where, p0, p1, p2, p3, weight, away, keep, rows):
    y, x = where[1], where[3]
    block = rows.shape[3]
    for j, piece in enumerate((p0, p1, p2, p3)):
        ay = lax.rem(y + j, 4)
        for low in range(2):
            ax = lax.rem(ay, 2) * 2 + low
            kx = lax.rem(ax + 4 - x, 4)
            for core in range(2):
                start = (core * 2 + low) * block
                rows[core, kx, lax.div(ay, 2)] = piece[start : start + block]

    @pl.loop(0, 2)
    def _(core):
        got = times(rows[core].reshape(-1, rows.shape[-1]), weight[...])

        @pl.when(core == 0)
        def _():
            keep[...] = got.reshape(keep.shape)

        @pl.when(core == 1)
        def _():
            away[...] = got.astype(BF16).reshape(away.shape)


def token_products(where, pieces, weight):
    token_rows, width = pieces[0].shape
    shape = (4, 2, token_rows // 4, weight.shape[0])
    return call(
        token_kernel,
        [(shape, BF16), (shape, F32)],
        [*pieces, weight],
        scratch=[pltpu.VMEM((2, 4, 2, token_rows // 4, width), BF16)],
        where=where,
        flops=8 * token_rows * width * width,
    )


def line_send_kernel(own, got, *outs):
    for k, out in enumerate(outs):
        out[...] = (own[k] + got[k].astype(F32)).astype(out.dtype)


def line_sends(own, got):
    shape = own.shape[1:]
    return call(line_send_kernel, [(shape, F32)] + [(shape, BF16)] * 3, [own, got])


def line_kernel(where, *refs):
    zh, zl = where[0], where[2]
    outs, sums = refs[8:12], refs[12]
    for plane in range(2):
        kept, one, two, three = refs[plane * 4 : plane * 4 + 4]
        sums[plane] = (
            kept[...] + one[...].astype(F32) + two[...].astype(F32) + three[...].astype(F32)
        )
    for k, out in enumerate(outs):
        az = lax.rem(zl + k, 4)
        plane = lax.rem(lax.div(az, 2) + zh, 2)
        out[...] = sums[plane, lax.rem(az, 2)].astype(out.dtype)


def line_sums(where, lines):
    block, width = lines[0].shape[1:]
    return call(
        line_kernel,
        [((block, width), F32)] + [((block, width), BF16)] * 3,
        lines,
        scratch=[pltpu.VMEM((2, 2, block, width), F32)],
        where=where,
    )


CHUNK = 384


def outer(lefts, rights, out, stage, sem, factor):
    dims = (((0,), (0,)), ((), ()))

    def send(i):
        start = pl.multiple_of(i * CHUNK, CHUNK)
        return pltpu.make_async_copy(stage.at[i], out.at[pl.ds(start, CHUNK)], sem.at[i])

    @pl.loop(0, out.shape[0] // CHUNK)
    def _(i):
        columns = pl.ds(pl.multiple_of(i * CHUNK, CHUNK), CHUNK)
        total = sum(
            lax.dot_general(left(columns), right(), dims, preferred_element_type=F32)
            for left, right in zip(lefts, rights)
        )
        stage[i] = (total * factor).astype(BF16)
        send(i).start()

    for i in range(out.shape[0] // CHUNK):
        send(i).wait()


def second_kernel(factor, where, *refs):
    pieces, (own, other, out, act, stage, sem) = refs[:4], refs[4:]
    rows = pieces[0].shape[1] // 2
    width = own.shape[-1]
    y = where[1]
    for i, piece in enumerate(pieces):

        @pl.loop(0, 4)
        def _(n):
            low, core = lax.div(n, 2), lax.rem(n, 2)
            ay = lax.bitwise_xor(y, i % 2 * 2 + low)
            block = core * 8 + i // 2 * 4 + lax.rem(ay + 4 - y, 4)
            values = piece[low, pl.ds(core * rows, rows)].astype(F32)
            act[pl.ds(block * rows, rows)] = gelu_value(values).astype(BF16)

    half = 8 * rows
    lefts = [lambda cols, n=n: act[n * half : (n + 1) * half, cols] for n in range(2)]
    rights = [lambda h=h: h[...].reshape(-1, width) for h in (own, other)]
    outer(lefts, rights, out, stage, sem, factor)


def first_kernel(factor, where, *refs):
    pieces, (own, other, out, right, stage, sem) = refs[:8], refs[8:]
    rows = pieces[0].shape[0] // 2
    half = 8 * rows
    for i, piece in enumerate(pieces):

        @pl.loop(0, 2)
        def _(core):
            right[pl.ds((core * 8 + i) * rows, rows)] = piece[pl.ds(core * rows, rows)]

    lefts = [
        lambda cols, h=h: h[:, :, :, :, cols].reshape(-1, CHUNK) for h in (own, other)
    ]
    rights = [lambda n=n: right[n * half : (n + 1) * half] for n in range(2)]
    outer(lefts, rights, out, stage, sem, factor)


def token_outer(kernel, where, pieces, halves, factor, swapped):
    width = pieces[0].shape[-1]
    tokens = sum(p.size for p in pieces) // width
    left, right = width, halves[0].shape[-1]
    if swapped:
        left, right = right, left
    return call(
        lambda *refs: kernel(factor, *refs),
        [((left, right), BF16)],
        [*pieces, *halves],
        scratch=[
            pltpu.VMEM((tokens, width), BF16),
            pltpu.VMEM((left // CHUNK, CHUNK, right), BF16),
            pltpu.SemaphoreType.DMA((left // CHUNK,)),
        ],
        where=where,
        flops=2 * tokens * left * right,
        hbm_out=True,
    )[0]


def compute(inputs, out_grad, preact, first_weight, second_weight):
    where = jnp.stack(
        [lax.axis_index(a) for a in ("zh", "y", "zl", "x", "c")]
    ).astype(jnp.int32)
    c = where[4]
    token_rows, width = preact.shape
    block = token_rows // 4
    factor = 1.0 / math.sqrt(8 * token_rows)

    split = preact.reshape(2, 2, block, width)
    preact = jnp.stack(
        [
            jnp.where(c == 0, split[:, 0], split[:, 1]),
            jnp.where(c == 0, split[:, 1], split[:, 0]),
        ]
    ).reshape(token_rows, width)

    grad_half = gather_shifts(where, out_grad)
    grad_other = swap(grad_half, "c")

    pre_near = jnp.stack([preact, flip(preact, "y", 1)])
    pre = [pre_near, flip(pre_near, "y", 2)]
    pre_far = swap(pre_near, "zh")
    pre += [pre_far, flip(pre_far, "y", 2)]

    part, first = own_act(grad_half, second_weight)

    def plane_sum(far):
        keep, *sends = other_act(far, grad_other, second_weight, part, first)
        got = [shift(s, "y", k) for k, s in zip((1, 2, 3), sends)]
        return keep + sum(g.astype(F32) for g in got)

    far_sum = plane_sum(1).astype(BF16)
    near_sum = plane_sum(0)
    from_far = swap(far_sum, "zh")
    grad_act = near_sum + from_far.astype(F32)
    grad_own = (grad_act * gelu_slope(preact.astype(F32))).astype(BF16)

    near = spread(grad_own)
    own_far = swap(grad_own, "zh")
    far = spread(own_far)

    def plane_inputs(pieces):
        away, keep = token_products(where, pieces, first_weight)
        got = swap(away, "c")
        keep, *sends = line_sends(keep, got)
        return [keep] + [shift(s, "x", k) for k, s in zip((1, 2, 3), sends)]

    lines = plane_inputs(near) + plane_inputs(far)
    grad_inputs, *sends = line_sums(where, lines)
    got = [shift(s, "zl", k) for k, s in zip((1, 2, 3), sends)]
    grad_inputs = grad_inputs + sum(g.astype(F32) for g in got)

    input_half = gather_flips(where, inputs)
    halves = (input_half, swap(input_half, "c"))
    grad_first = token_outer(first_kernel, where, near + far, halves, factor, True)
    grad_second = token_outer(
        second_kernel, where, pre, (grad_half, grad_other), factor, False
    )
    return (grad_inputs, grad_first, grad_second)


def solution(mesh):
    fine = Mesh(mesh.devices.reshape(2, 4, 4, 4, 2), ("zh", "y", "zl", "x", "c"))
    row, col = ("zh", "y"), ("zl", "x", "c")
    return jax.shard_map(
        compute,
        mesh=fine,
        in_specs=(P(col, row), P(col, row), P(row, col), P(row, col), P(col, row)),
        out_specs=(P(col, row), P(row, col), P(col, row)),
        check_vma=False,
    )
```

```python
import math

import jax
import jax.numpy as jnp
from jax import lax
from jax.experimental import pallas as pl
from jax.experimental.pallas import tpu as pltpu
from jax.sharding import Mesh
from jax.sharding import PartitionSpec as P


INV_ROOT_TWO = 0.7071067811865476
INV_ROOT_TWO_PI = 0.3989422804014327
BF16 = jnp.bfloat16
F32 = jnp.float32


def gelu_value(values):
    return 0.5 * values * (1.0 + lax.erf(values * INV_ROOT_TWO))


def gelu_slope(values):
    normal_cdf = 0.5 * (1.0 + lax.erf(values * INV_ROOT_TWO))
    density = jnp.exp(-0.5 * values * values) * INV_ROOT_TWO_PI
    return normal_cdf + values * density


def shift(value, axis, step):
    size = lax.axis_size(axis)
    return lax.ppermute(value, axis, [(i, (i + step) % size) for i in range(size)])


def flip(value, axis, mask):
    size = lax.axis_size(axis)
    return lax.ppermute(value, axis, [(i, i ^ mask) for i in range(size)])


def swap(value, axis):
    return lax.ppermute(value, axis, [(0, 1), (1, 0)])


VMEM = pl.BlockSpec(memory_space=pltpu.VMEM)
SMEM = pl.BlockSpec(memory_space=pltpu.SMEM)


def cost(flops, moved):
    return pl.CostEstimate(flops=flops, bytes_accessed=moved, transcendentals=0)


def call(kernel, outs, operands, scratch=(), where=None, flops=0, hbm_out=False):
    moved = sum(2 * o.size for o in operands)
    operands = [pltpu.with_memory_space_constraint(o, pltpu.VMEM) for o in operands]
    specs = [VMEM] * len(operands)
    if where is not None:
        operands, specs = [where] + operands, [SMEM] + specs
    space = pl.BlockSpec(memory_space=pl.ANY) if hbm_out else VMEM
    make = jax.ShapeDtypeStruct if hbm_out else pltpu.VMEM
    return pl.pallas_call(
        kernel,
        out_shape=tuple(make(shape, dtype) for shape, dtype in outs),
        in_specs=specs,
        out_specs=(space,) * len(outs),
        scratch_shapes=scratch,
        cost_estimate=cost(flops, moved),
        compiler_params=pltpu.CompilerParams(vmem_limit_bytes=GRANT),
    )(*operands)


GRANT = 12 * 1024 * 1024


def times(left, right):
    return lax.dot_general(left, right, (((1,), (1,)), ((), ())), preferred_element_type=F32)


def place(where, out, az, ax, block):
    zh, y = where[0], where[1]
    far = lax.rem(lax.div(az, 2) + zh, 2)
    ay = lax.rem(az, 2) * 2 + lax.div(ax, 2)
    out[far, lax.rem(ay + 4 - y, 4), lax.rem(ax, 2)] = block


def shift_place_kernel(where, *refs):
    for kz in range(4):
        for kx in range(4):
            az = lax.rem(where[2] + 4 - kz, 4)
            ax = lax.rem(where[3] + 4 - kx, 4)
            place(where, refs[-1], az, ax, refs[kx][kz])


def flip_place_kernel(where, near, far, out):
    for kz in range(4):
        for kx in range(4):
            az = lax.bitwise_xor(where[2], kz)
            ax = lax.bitwise_xor(where[3], kx)
            place(where, out, az, ax, (near, far)[kx // 2][kx % 2, kz])


def col_place(kernel, where, pieces):
    rows, width = pieces[0].shape[-2:]
    return call(kernel, [((2, 4, 2, rows, width), BF16)], pieces, where=where)[0]


def shifts(value, axis):
    got = [value]
    for k in (1, 2, 3):
        got.append(shift(value, axis, k))
    return got


def spread(value):
    own, one, two, three = shifts(value, "y")
    return [own, three, two, one]


def gather_shifts(where, own):
    line = jnp.stack(shifts(own, "zl"))
    return col_place(shift_place_kernel, where, shifts(line, "x"))


def gather_flips(where, own):
    pair = jnp.stack([own, flip(own, "zl", 1)])
    line = jnp.concatenate([pair, flip(pair, "zl", 2)])
    lines = jnp.stack([line, flip(line, "x", 1)])
    rest = flip(lines, "x", 2)
    return col_place(flip_place_kernel, where, [lines, rest])


def own_act_kernel(half, weight, part, first):
    @pl.loop(0, 2)
    def _(far):
        rows = half[far].reshape(-1, half.shape[-1])
        got = times(rows, weight[...]).reshape(part.shape[1:])
        part[far] = got.astype(BF16)
        first[far] = got[0]


def own_act(half, weight):
    width = weight.shape[0]
    rows = half.shape[2] * half.shape[3]
    return call(
        own_act_kernel,
        [((2, 4, rows, width), BF16), ((2, rows, width), F32)],
        [half, weight],
        flops=2 * half.size * width,
    )


def other_act_kernel(far, half, weight, part, first, keep, one, two, three):
    rows = part.shape[2]
    got = times(half[far].reshape(-1, half.shape[-1]), weight[...])
    keep[:rows] = first[far]
    keep[rows:] = got[:rows]
    for k, send in ((1, one), (2, two), (3, three)):
        send[:rows] = part[far, k]
        send[rows:] = got[k * rows : (k + 1) * rows].astype(BF16)


def other_act(far, half, weight, part, first):
    width = weight.shape[0]
    rows = 2 * part.shape[2]
    return call(
        lambda *refs: other_act_kernel(far, *refs),
        [((rows, width), F32)] + [((rows, width), BF16)] * 3,
        [half, weight, part, first],
        flops=half.size * width,
    )


def token_kernel(where, p0, p1, p2, p3, weight, away, keep, rows):
    y, x = where[1], where[3]
    block = rows.shape[3]
    for j, piece in enumerate((p0, p1, p2, p3)):
        ay = lax.rem(y + j, 4)
        for low in range(2):
            ax = lax.rem(ay, 2) * 2 + low
            kx = lax.rem(ax + 4 - x, 4)
            for core in range(2):
                start = (core * 2 + low) * block
                rows[core, kx, lax.div(ay, 2)] = piece[start : start + block]

    @pl.loop(0, 2)
    def _(core):
        got = times(rows[core].reshape(-1, rows.shape[-1]), weight[...])

        @pl.when(core == 0)
        def _():
            keep[...] = got.reshape(keep.shape)

        @pl.when(core == 1)
        def _():
            away[...] = got.astype(BF16).reshape(away.shape)


def token_products(where, pieces, weight):
    token_rows, width = pieces[0].shape
    shape = (4, 2, token_rows // 4, weight.shape[0])
    return call(
        token_kernel,
        [(shape, BF16), (shape, F32)],
        [*pieces, weight],
        scratch=[pltpu.VMEM((2, 4, 2, token_rows // 4, width), BF16)],
        where=where,
        flops=8 * token_rows * width * width,
    )


def line_send_kernel(own, got, *outs):
    for k, out in enumerate(outs):
        out[...] = (own[k] + got[k].astype(F32)).astype(out.dtype)


def line_sends(own, got):
    shape = own.shape[1:]
    return call(line_send_kernel, [(shape, F32)] + [(shape, BF16)] * 3, [own, got])


def line_kernel(where, *refs):
    zh, zl = where[0], where[2]
    outs, sums = refs[8:12], refs[12]
    for plane in range(2):
        kept, one, two, three = refs[plane * 4 : plane * 4 + 4]
        sums[plane] = (
            kept[...] + one[...].astype(F32) + two[...].astype(F32) + three[...].astype(F32)
        )
    for k, out in enumerate(outs):
        az = lax.rem(zl + k, 4)
        plane = lax.rem(lax.div(az, 2) + zh, 2)
        out[...] = sums[plane, lax.rem(az, 2)].astype(out.dtype)


def line_sums(where, lines):
    block, width = lines[0].shape[1:]
    return call(
        line_kernel,
        [((block, width), F32)] + [((block, width), BF16)] * 3,
        lines,
        scratch=[pltpu.VMEM((2, 2, block, width), F32)],
        where=where,
    )


CHUNK = 384


def outer(lefts, rights, columns_total, emit):
    dims = (((0,), (0,)), ((), ()))

    @pl.loop(0, columns_total // CHUNK)
    def _(i):
        columns = pl.ds(pl.multiple_of(i * CHUNK, CHUNK), CHUNK)
        total = sum(
            lax.dot_general(left(columns), right(), dims, preferred_element_type=F32)
            for left, right in zip(lefts, rights)
        )
        emit(i, columns, total)


def store_out(out, stage, sem, factor):
    def send(i):
        rows = pl.ds(pl.multiple_of(i * CHUNK, CHUNK), CHUNK)
        return pltpu.make_async_copy(stage.at[i], out.at[rows], sem.at[i])

    def emit(i, total):
        stage[i] = (total * factor).astype(BF16)
        send(i).start()

    def finish():
        for i in range(out.shape[0] // CHUNK):
            send(i).wait()

    return emit, finish


def stage_scratch(rows, width):
    return [
        pltpu.VMEM((rows // CHUNK, CHUNK, width), BF16),
        pltpu.SemaphoreType.DMA((rows // CHUNK,)),
    ]


def second_kernel(plane, factor, where, *refs):
    pieces, (own, other), refs = refs[:2], refs[2:4], refs[4:]
    rows = pieces[0].shape[1] // 2
    width = own.shape[-1]
    act = refs[2] if plane else refs[1]
    y = where[1]
    for high, piece in enumerate(pieces):

        @pl.loop(0, 4)
        def _(n):
            low, core = lax.div(n, 2), lax.rem(n, 2)
            ay = lax.bitwise_xor(y, high * 2 + low)
            block = core * 4 + lax.rem(ay + 4 - y, 4)
            values = piece[low, pl.ds(core * rows, rows)].astype(F32)
            act[pl.ds(block * rows, rows)] = gelu_value(values).astype(BF16)

    half = 4 * rows
    lefts = [lambda cols, n=n: act[n * half : (n + 1) * half, cols] for n in range(2)]
    rights = [lambda h=h: h[plane].reshape(-1, width) for h in (own, other)]
    if plane:
        so_far, out, _, stage, sem = refs
        emit, finish = store_out(out, stage, sem, factor)
        outer(
            lefts, rights, act.shape[1], lambda i, cols, t: emit(i, t + so_far[cols])
        )
        finish()
    else:
        total = refs[0]

        def keep(i, cols, value):
            total[cols] = value

        outer(lefts, rights, act.shape[1], keep)


def second_product(where, near, far, halves, factor):
    rows, width = near[0].shape[1:]
    out_width = halves[0].shape[-1]
    flops = 8 * rows * width * out_width
    act = pltpu.VMEM((4 * rows, width), BF16)
    (total,) = call(
        lambda *refs: second_kernel(0, factor, *refs),
        [((width, out_width), F32)],
        [*near, *halves],
        scratch=[act],
        where=where,
        flops=flops,
    )
    return call(
        lambda *refs: second_kernel(1, factor, *refs),
        [((width, out_width), BF16)],
        [*far, *halves, total],
        scratch=[act, *stage_scratch(width, out_width)],
        where=where,
        flops=flops,
        hbm_out=True,
    )[0]


def first_kernel(factor, *refs):
    pieces, (own, other, out, right, stage, sem) = refs[:8], refs[8:]
    rows = pieces[0].shape[0] // 2
    half = 8 * rows
    for i, piece in enumerate(pieces):

        @pl.loop(0, 2)
        def _(core):
            right[pl.ds((core * 8 + i) * rows, rows)] = piece[pl.ds(core * rows, rows)]

    lefts = [
        lambda cols, h=h: h[:, :, :, :, cols].reshape(-1, CHUNK) for h in (own, other)
    ]
    rights = [lambda n=n: right[n * half : (n + 1) * half] for n in range(2)]
    emit, finish = store_out(out, stage, sem, factor)
    outer(lefts, rights, out.shape[0], lambda i, cols, t: emit(i, t))
    finish()


def first_product(pieces, halves, factor):
    rows, width = pieces[0].shape
    out_rows = halves[0].shape[-1]
    return call(
        lambda *refs: first_kernel(factor, *refs),
        [((out_rows, width), BF16)],
        [*pieces, *halves],
        scratch=[pltpu.VMEM((8 * rows, width), BF16), *stage_scratch(out_rows, width)],
        flops=16 * rows * width * out_rows,
        hbm_out=True,
    )[0]


def compute(inputs, out_grad, preact, first_weight, second_weight):
    where = jnp.stack(
        [lax.axis_index(a) for a in ("zh", "y", "zl", "x", "c")]
    ).astype(jnp.int32)
    c = where[4]
    token_rows, width = preact.shape
    block = token_rows // 4
    factor = 1.0 / math.sqrt(8 * token_rows)

    split = preact.reshape(2, 2, block, width)
    preact = jnp.stack(
        [
            jnp.where(c == 0, split[:, 0], split[:, 1]),
            jnp.where(c == 0, split[:, 1], split[:, 0]),
        ]
    ).reshape(token_rows, width)

    grad_half = gather_shifts(where, out_grad)
    grad_other = swap(grad_half, "c")

    pre_near = jnp.stack([preact, flip(preact, "y", 1)])
    pre = [pre_near, flip(pre_near, "y", 2)]
    pre_far = swap(pre_near, "zh")
    pre += [pre_far, flip(pre_far, "y", 2)]

    part, first = own_act(grad_half, second_weight)

    def plane_sum(far):
        keep, *sends = other_act(far, grad_other, second_weight, part, first)
        got = [shift(s, "y", k) for k, s in zip((1, 2, 3), sends)]
        return keep + sum(g.astype(F32) for g in got)

    far_sum = plane_sum(1).astype(BF16)
    near_sum = plane_sum(0)
    from_far = swap(far_sum, "zh")
    grad_act = near_sum + from_far.astype(F32)
    grad_own = (grad_act * gelu_slope(preact.astype(F32))).astype(BF16)

    near = spread(grad_own)
    own_far = swap(grad_own, "zh")
    far = spread(own_far)

    def plane_inputs(pieces):
        away, keep = token_products(where, pieces, first_weight)
        got = swap(away, "c")
        keep, *sends = line_sends(keep, got)
        return [keep] + [shift(s, "x", k) for k, s in zip((1, 2, 3), sends)]

    lines = plane_inputs(near) + plane_inputs(far)
    grad_inputs, *sends = line_sums(where, lines)
    got = [shift(s, "zl", k) for k, s in zip((1, 2, 3), sends)]
    grad_inputs = grad_inputs + sum(g.astype(F32) for g in got)

    input_half = gather_flips(where, inputs)
    halves = (input_half, swap(input_half, "c"))
    grad_first = first_product(near + far, halves, factor)
    grad_second = second_product(
        where, pre[:2], pre[2:], (grad_half, grad_other), factor
    )
    return (grad_inputs, grad_first, grad_second)


def solution(mesh):
    fine = Mesh(mesh.devices.reshape(2, 4, 4, 4, 2), ("zh", "y", "zl", "x", "c"))
    row, col = ("zh", "y"), ("zl", "x", "c")
    return jax.shard_map(
        compute,
        mesh=fine,
        in_specs=(P(col, row), P(col, row), P(row, col), P(row, col), P(col, row)),
        out_specs=(P(col, row), P(row, col), P(col, row)),
        check_vma=False,
    )
```

```python
import math

import jax
import jax.numpy as jnp
from jax import lax
from jax.experimental import pallas as pl
from jax.experimental.pallas import tpu as pltpu
from jax.sharding import Mesh
from jax.sharding import PartitionSpec as P


INV_ROOT_TWO = 0.7071067811865476
INV_ROOT_TWO_PI = 0.3989422804014327
BF16 = jnp.bfloat16
F32 = jnp.float32


def gelu_value(values):
    return 0.5 * values * (1.0 + lax.erf(values * INV_ROOT_TWO))


def gelu_slope(values):
    normal_cdf = 0.5 * (1.0 + lax.erf(values * INV_ROOT_TWO))
    density = jnp.exp(-0.5 * values * values) * INV_ROOT_TWO_PI
    return normal_cdf + values * density


def shift(value, axis, step):
    size = lax.axis_size(axis)
    return lax.ppermute(value, axis, [(i, (i + step) % size) for i in range(size)])


def flip(value, axis, mask):
    size = lax.axis_size(axis)
    return lax.ppermute(value, axis, [(i, i ^ mask) for i in range(size)])


def swap(value, axis):
    return lax.ppermute(value, axis, [(0, 1), (1, 0)])


VMEM = pl.BlockSpec(memory_space=pltpu.VMEM)
SMEM = pl.BlockSpec(memory_space=pltpu.SMEM)


def cost(flops, moved):
    return pl.CostEstimate(flops=flops, bytes_accessed=moved, transcendentals=0)


def call(kernel, outs, operands, scratch=(), where=None, flops=0, hbm_out=False):
    moved = sum(2 * o.size for o in operands)
    operands = [pltpu.with_memory_space_constraint(o, pltpu.VMEM) for o in operands]
    specs = [VMEM] * len(operands)
    if where is not None:
        operands, specs = [where] + operands, [SMEM] + specs
    space = pl.BlockSpec(memory_space=pl.ANY) if hbm_out else VMEM
    make = jax.ShapeDtypeStruct if hbm_out else pltpu.VMEM
    return pl.pallas_call(
        kernel,
        out_shape=tuple(make(shape, dtype) for shape, dtype in outs),
        in_specs=specs,
        out_specs=(space,) * len(outs),
        scratch_shapes=scratch,
        cost_estimate=cost(flops, moved),
        compiler_params=pltpu.CompilerParams(vmem_limit_bytes=GRANT),
    )(*operands)


GRANT = 12 * 1024 * 1024


def times(left, right):
    return lax.dot_general(left, right, (((1,), (1,)), ((), ())), preferred_element_type=F32)


def place_kernel(where, *refs):
    out = refs[-1]
    zh, y, zl, x = (where[i] for i in range(4))
    for kz in range(4):
        for kx in range(4):
            az = lax.rem(zl + 4 - kz, 4)
            ax = lax.rem(x + 4 - kx, 4)
            far = lax.rem(lax.div(az, 2) + zh, 2)
            ay = lax.rem(az, 2) * 2 + lax.div(ax, 2)
            out[far, lax.rem(ay + 4 - y, 4), lax.rem(ax, 2)] = refs[kx][kz]


def shifts(value, axis):
    got = [value]
    for k in (1, 2, 3):
        got.append(shift(value, axis, k))
    return got


def spread(value):
    own, one, two, three = shifts(value, "y")
    return [own, three, two, one]


def core_gather(where, own):
    line = jnp.stack(shifts(own, "zl"))
    pieces = shifts(line, "x")
    rows, width = own.shape
    out = ((2, 4, 2, rows, width), BF16)
    return call(place_kernel, [out], pieces, where=where)[0]


def own_act_kernel(half, weight, part, first):
    @pl.loop(0, 2)
    def _(far):
        rows = half[far].reshape(-1, half.shape[-1])
        got = times(rows, weight[...]).reshape(part.shape[1:])
        part[far] = got.astype(BF16)
        first[far] = got[0]


def own_act(half, weight):
    width = weight.shape[0]
    rows = half.shape[2] * half.shape[3]
    return call(
        own_act_kernel,
        [((2, 4, rows, width), BF16), ((2, rows, width), F32)],
        [half, weight],
        flops=2 * half.size * width,
    )


def other_act_kernel(far, half, weight, part, first, keep, one, two, three):
    rows = part.shape[2]
    got = times(half[far].reshape(-1, half.shape[-1]), weight[...])
    keep[:rows] = first[far]
    keep[rows:] = got[:rows]
    for k, send in ((1, one), (2, two), (3, three)):
        send[:rows] = part[far, k]
        send[rows:] = got[k * rows : (k + 1) * rows].astype(BF16)


def other_act(far, half, weight, part, first):
    width = weight.shape[0]
    rows = 2 * part.shape[2]
    return call(
        lambda *refs: other_act_kernel(far, *refs),
        [((rows, width), F32)] + [((rows, width), BF16)] * 3,
        [half, weight, part, first],
        flops=half.size * width,
    )


def token_kernel(where, p0, p1, p2, p3, weight, away, keep, rows):
    y, x = where[1], where[3]
    block = rows.shape[3]
    for j, piece in enumerate((p0, p1, p2, p3)):
        ay = lax.rem(y + j, 4)
        for low in range(2):
            ax = lax.rem(ay, 2) * 2 + low
            kx = lax.rem(ax + 4 - x, 4)
            for core in range(2):
                start = (core * 2 + low) * block
                rows[core, kx, lax.div(ay, 2)] = piece[start : start + block]

    @pl.loop(0, 2)
    def _(core):
        got = times(rows[core].reshape(-1, rows.shape[-1]), weight[...])

        @pl.when(core == 0)
        def _():
            keep[...] = got.reshape(keep.shape)

        @pl.when(core == 1)
        def _():
            away[...] = got.astype(BF16).reshape(away.shape)


def token_products(where, pieces, weight):
    token_rows, width = pieces[0].shape
    shape = (4, 2, token_rows // 4, weight.shape[0])
    return call(
        token_kernel,
        [(shape, BF16), (shape, F32)],
        [*pieces, weight],
        scratch=[pltpu.VMEM((2, 4, 2, token_rows // 4, width), BF16)],
        where=where,
        flops=8 * token_rows * width * width,
    )


def line_send_kernel(own, got, *outs):
    for k, out in enumerate(outs):
        out[...] = (own[k] + got[k].astype(F32)).astype(out.dtype)


def line_sends(own, got):
    shape = own.shape[1:]
    return call(line_send_kernel, [(shape, F32)] + [(shape, BF16)] * 3, [own, got])


def line_kernel(where, *refs):
    zh, zl = where[0], where[2]
    outs, sums = refs[8:12], refs[12]
    for plane in range(2):
        kept, one, two, three = refs[plane * 4 : plane * 4 + 4]
        sums[plane] = (
            kept[...] + one[...].astype(F32) + two[...].astype(F32) + three[...].astype(F32)
        )
    for k, out in enumerate(outs):
        az = lax.rem(zl + k, 4)
        plane = lax.rem(lax.div(az, 2) + zh, 2)
        out[...] = sums[plane, lax.rem(az, 2)].astype(out.dtype)


def line_sums(where, lines):
    block, width = lines[0].shape[1:]
    return call(
        line_kernel,
        [((block, width), F32)] + [((block, width), BF16)] * 3,
        lines,
        scratch=[pltpu.VMEM((2, 2, block, width), F32)],
        where=where,
    )


CHUNK = 384


def outer(lefts, rights, columns_total, emit):
    dims = (((0,), (0,)), ((), ()))

    @pl.loop(0, columns_total // CHUNK)
    def _(i):
        columns = pl.ds(pl.multiple_of(i * CHUNK, CHUNK), CHUNK)
        total = sum(
            lax.dot_general(left(columns), right(), dims, preferred_element_type=F32)
            for left, right in zip(lefts, rights)
        )
        emit(i, columns, total)


def store_out(out, stage, sem, factor):
    def send(i):
        rows = pl.ds(pl.multiple_of(i * CHUNK, CHUNK), CHUNK)
        return pltpu.make_async_copy(stage.at[i], out.at[rows], sem.at[i])

    def emit(i, total):
        stage[i] = (total * factor).astype(BF16)
        send(i).start()

    def finish():
        for i in range(out.shape[0] // CHUNK):
            send(i).wait()

    return emit, finish


def stage_scratch(rows, width):
    return [
        pltpu.VMEM((rows // CHUNK, CHUNK, width), BF16),
        pltpu.SemaphoreType.DMA((rows // CHUNK,)),
    ]


def second_kernel(plane, factor, where, *refs):
    pieces, (own, other), refs = refs[:2], refs[2:4], refs[4:]
    rows = pieces[0].shape[1] // 2
    width = own.shape[-1]
    act = refs[2] if plane else refs[1]
    y = where[1]
    for high, piece in enumerate(pieces):

        @pl.loop(0, 4)
        def _(n):
            low, core = lax.div(n, 2), lax.rem(n, 2)
            ay = lax.bitwise_xor(y, high * 2 + low)
            block = core * 4 + lax.rem(ay + 4 - y, 4)
            values = piece[low, pl.ds(core * rows, rows)].astype(F32)
            act[pl.ds(block * rows, rows)] = gelu_value(values).astype(BF16)

    half = 4 * rows
    lefts = [lambda cols, n=n: act[n * half : (n + 1) * half, cols] for n in range(2)]
    rights = [lambda h=h: h[plane].reshape(-1, width) for h in (own, other)]
    if plane:
        so_far, out, _, stage, sem = refs
        emit, finish = store_out(out, stage, sem, factor)
        outer(
            lefts, rights, act.shape[1], lambda i, cols, t: emit(i, t + so_far[cols])
        )
        finish()
    else:
        total = refs[0]

        def keep(i, cols, value):
            total[cols] = value

        outer(lefts, rights, act.shape[1], keep)


def second_product(where, near, far, halves, factor):
    rows, width = near[0].shape[1:]
    out_width = halves[0].shape[-1]
    flops = 8 * rows * width * out_width
    act = pltpu.VMEM((4 * rows, width), BF16)
    (total,) = call(
        lambda *refs: second_kernel(0, factor, *refs),
        [((width, out_width), F32)],
        [*near, *halves],
        scratch=[act],
        where=where,
        flops=flops,
    )
    return call(
        lambda *refs: second_kernel(1, factor, *refs),
        [((width, out_width), BF16)],
        [*far, *halves, total],
        scratch=[act, *stage_scratch(width, out_width)],
        where=where,
        flops=flops,
        hbm_out=True,
    )[0]


def first_kernel(factor, *refs):
    pieces, (own, other, out, right, stage, sem) = refs[:8], refs[8:]
    rows = pieces[0].shape[0] // 2
    half = 8 * rows
    for i, piece in enumerate(pieces):

        @pl.loop(0, 2)
        def _(core):
            right[pl.ds((core * 8 + i) * rows, rows)] = piece[pl.ds(core * rows, rows)]

    lefts = [
        lambda cols, h=h: h[:, :, :, :, cols].reshape(-1, CHUNK) for h in (own, other)
    ]
    rights = [lambda n=n: right[n * half : (n + 1) * half] for n in range(2)]
    emit, finish = store_out(out, stage, sem, factor)
    outer(lefts, rights, out.shape[0], lambda i, cols, t: emit(i, t))
    finish()


def first_product(pieces, halves, factor):
    rows, width = pieces[0].shape
    out_rows = halves[0].shape[-1]
    return call(
        lambda *refs: first_kernel(factor, *refs),
        [((out_rows, width), BF16)],
        [*pieces, *halves],
        scratch=[pltpu.VMEM((8 * rows, width), BF16), *stage_scratch(out_rows, width)],
        flops=16 * rows * width * out_rows,
        hbm_out=True,
    )[0]


def compute(inputs, out_grad, preact, first_weight, second_weight):
    where = jnp.stack(
        [lax.axis_index(a) for a in ("zh", "y", "zl", "x", "c")]
    ).astype(jnp.int32)
    c = where[4]
    token_rows, width = preact.shape
    block = token_rows // 4
    factor = 1.0 / math.sqrt(8 * token_rows)

    split = preact.reshape(2, 2, block, width)
    preact = jnp.stack(
        [
            jnp.where(c == 0, split[:, 0], split[:, 1]),
            jnp.where(c == 0, split[:, 1], split[:, 0]),
        ]
    ).reshape(token_rows, width)

    grad_half = core_gather(where, out_grad)
    grad_other = swap(grad_half, "c")

    pre_near = jnp.stack([preact, flip(preact, "y", 1)])
    pre = [pre_near, flip(pre_near, "y", 2)]
    pre_far = swap(pre_near, "zh")
    pre += [pre_far, flip(pre_far, "y", 2)]

    part, first = own_act(grad_half, second_weight)

    def plane_sum(far):
        keep, *sends = other_act(far, grad_other, second_weight, part, first)
        got = [shift(s, "y", k) for k, s in zip((1, 2, 3), sends)]
        return keep + sum(g.astype(F32) for g in got)

    far_sum = plane_sum(1).astype(BF16)
    near_sum = plane_sum(0)
    from_far = swap(far_sum, "zh")
    grad_act = near_sum + from_far.astype(F32)
    grad_own = (grad_act * gelu_slope(preact.astype(F32))).astype(BF16)

    near = spread(grad_own)
    own_far = swap(grad_own, "zh")
    far = spread(own_far)

    def plane_inputs(pieces):
        away, keep = token_products(where, pieces, first_weight)
        got = swap(away, "c")
        keep, *sends = line_sends(keep, got)
        return [keep] + [shift(s, "x", k) for k, s in zip((1, 2, 3), sends)]

    lines = plane_inputs(near) + plane_inputs(far)
    grad_inputs, *sends = line_sums(where, lines)
    got = [shift(s, "zl", k) for k, s in zip((1, 2, 3), sends)]
    grad_inputs = grad_inputs + sum(g.astype(F32) for g in got)

    input_half = core_gather(where, inputs)
    halves = (input_half, swap(input_half, "c"))
    grad_first = first_product(near + far, halves, factor)
    grad_second = second_product(
        where, pre[:2], pre[2:], (grad_half, grad_other), factor
    )
    return (grad_inputs, grad_first, grad_second)


def solution(mesh):
    fine = Mesh(mesh.devices.reshape(2, 4, 4, 4, 2), ("zh", "y", "zl", "x", "c"))
    row, col = ("zh", "y"), ("zl", "x", "c")
    return jax.shard_map(
        compute,
        mesh=fine,
        in_specs=(P(col, row), P(col, row), P(row, col), P(row, col), P(col, row)),
        out_specs=(P(col, row), P(row, col), P(col, row)),
        check_vma=False,
    )
```

```python
import math

import jax
import jax.numpy as jnp
from jax import lax
from jax.experimental import pallas as pl
from jax.experimental.pallas import tpu as pltpu
from jax.sharding import Mesh
from jax.sharding import PartitionSpec as P


INV_ROOT_TWO = 0.7071067811865476
INV_ROOT_TWO_PI = 0.3989422804014327
BF16 = jnp.bfloat16
F32 = jnp.float32


def gelu_value(values):
    return 0.5 * values * (1.0 + lax.erf(values * INV_ROOT_TWO))


def gelu_slope(values):
    normal_cdf = 0.5 * (1.0 + lax.erf(values * INV_ROOT_TWO))
    density = jnp.exp(-0.5 * values * values) * INV_ROOT_TWO_PI
    return normal_cdf + values * density


def shift(value, axis, step):
    size = lax.axis_size(axis)
    return lax.ppermute(value, axis, [(i, (i + step) % size) for i in range(size)])


def flip(value, axis, mask):
    size = lax.axis_size(axis)
    return lax.ppermute(value, axis, [(i, i ^ mask) for i in range(size)])


def swap(value, axis):
    return lax.ppermute(value, axis, [(0, 1), (1, 0)])


VMEM = pl.BlockSpec(memory_space=pltpu.VMEM)
SMEM = pl.BlockSpec(memory_space=pltpu.SMEM)


def cost(flops, moved):
    return pl.CostEstimate(flops=flops, bytes_accessed=moved, transcendentals=0)


def call(kernel, outs, operands, scratch=(), where=None, flops=0, hbm_out=False):
    moved = sum(2 * o.size for o in operands)
    operands = [pltpu.with_memory_space_constraint(o, pltpu.VMEM) for o in operands]
    specs = [VMEM] * len(operands)
    if where is not None:
        operands, specs = [where] + operands, [SMEM] + specs
    space = pl.BlockSpec(memory_space=pl.ANY) if hbm_out else VMEM
    make = jax.ShapeDtypeStruct if hbm_out else pltpu.VMEM
    return pl.pallas_call(
        kernel,
        out_shape=tuple(make(shape, dtype) for shape, dtype in outs),
        in_specs=specs,
        out_specs=(space,) * len(outs),
        scratch_shapes=scratch,
        cost_estimate=cost(flops, moved),
        compiler_params=pltpu.CompilerParams(vmem_limit_bytes=GRANT),
    )(*operands)


GRANT = 12 * 1024 * 1024


def times(left, right):
    return lax.dot_general(left, right, (((1,), (1,)), ((), ())), preferred_element_type=F32)


def place_kernel(where, *refs):
    out = refs[-1]
    y, zl, x = (where[i] for i in range(1, 4))

    @pl.loop(0, 4)
    def _(kz):
        az = lax.rem(zl + 4 - kz, 4)
        for kx in range(4):
            ax = lax.rem(x + 4 - kx, 4)
            ay = lax.rem(az, 2) * 2 + lax.div(ax, 2)
            out[lax.div(az, 2), lax.rem(ay + 4 - y, 4), lax.rem(ax, 2)] = refs[kx][kz]


def shifts(value, axis):
    got = [value]
    for k in (1, 2, 3):
        got.append(shift(value, axis, k))
    return got


def spread(value):
    own, one, two, three = shifts(value, "y")
    return [own, three, two, one]


def core_gather(where, own):
    pieces = shifts(own, "zl")
    line = jnp.stack(pieces)
    pieces = shifts(line, "x")
    rows, width = own.shape
    out = ((2, 4, 2, rows, width), BF16)
    return call(place_kernel, [out], pieces, where=where)[0]


def own_act_kernel(half, weight, part, first):
    @pl.loop(0, 2)
    def _(far):
        rows = half[far].reshape(-1, half.shape[-1])
        got = times(rows, weight[...]).reshape(part.shape[1:])
        part[far] = got.astype(BF16)
        first[far] = got[0]


def own_act(half, weight):
    width = weight.shape[0]
    rows = half.shape[2] * half.shape[3]
    return call(
        own_act_kernel,
        [((2, 4, rows, width), BF16), ((2, rows, width), F32)],
        [half, weight],
        flops=2 * half.size * width,
    )


def other_act_kernel(far, half, weight, part, first, keep, one, two, three):
    rows = part.shape[2]
    got = times(half[far].reshape(-1, half.shape[-1]), weight[...])
    keep[:rows] = first[far]
    keep[rows:] = got[:rows]
    for k, send in ((1, one), (2, two), (3, three)):
        send[:rows] = part[far, k]
        send[rows:] = got[k * rows : (k + 1) * rows].astype(BF16)


def other_act(far, half, weight, part, first):
    width = weight.shape[0]
    rows = 2 * part.shape[2]
    return call(
        lambda *refs: other_act_kernel(far, *refs),
        [((rows, width), F32)] + [((rows, width), BF16)] * 3,
        [half, weight, part, first],
        flops=half.size * width,
    )


ROWS = 16


def row_sum_kernel(keep, one, two, three, total, send):
    @pl.loop(0, keep.shape[0] // ROWS)
    def _(i):
        r = pl.ds(pl.multiple_of(i * ROWS, ROWS), ROWS)
        value = (
            keep[r] + one[r].astype(F32) + two[r].astype(F32) + three[r].astype(F32)
        )
        total[r] = value
        send[r] = value.astype(BF16)


def row_sum(keep, got):
    return call(row_sum_kernel, [(keep.shape, F32), (keep.shape, BF16)], [keep, *got])


def hidden_kernel(plane, where, total, got, near, far, out):
    @pl.loop(0, total.shape[0] // ROWS)
    def _(i):
        r = pl.ds(pl.multiple_of(i * ROWS, ROWS), ROWS)
        values = jnp.where(where[0] == plane, near[r].astype(F32), far[0, r].astype(F32))
        grad_act = total[r] + got[r].astype(F32)
        out[r] = (grad_act * gelu_slope(values)).astype(BF16)


def hidden(plane, where, total, got, near, far):
    return call(
        lambda *refs: hidden_kernel(plane, *refs),
        [(total.shape, BF16)],
        [total, got, near, far],
        where=where,
    )[0]


def token_kernel(where, p0, p1, p2, p3, weight, away, keep, rows):
    y, x = where[1], where[3]
    block = rows.shape[3]
    for j, piece in enumerate((p0, p1, p2, p3)):
        ay = lax.rem(y + j, 4)
        for low in range(2):
            ax = lax.rem(ay, 2) * 2 + low
            kx = lax.rem(ax + 4 - x, 4)

            @pl.loop(0, 2)
            def _(core):
                start = pl.multiple_of((core * 2 + low) * block, block)
                rows[core, kx, lax.div(ay, 2)] = piece[pl.ds(start, block)]

    @pl.loop(0, 2)
    def _(core):
        got = times(rows[core].reshape(-1, rows.shape[-1]), weight[...])

        @pl.when(core == 0)
        def _():
            keep[...] = got.reshape(keep.shape)

        @pl.when(core == 1)
        def _():
            away[...] = got.astype(BF16).reshape(away.shape)


def token_products(where, pieces, weight):
    token_rows, width = pieces[0].shape
    shape = (4, 2, token_rows // 4, weight.shape[0])
    return call(
        token_kernel,
        [(shape, BF16), (shape, F32)],
        [*pieces, weight],
        scratch=[pltpu.VMEM((2, 4, 2, token_rows // 4, width), BF16)],
        where=where,
        flops=8 * token_rows * width * width,
    )


def line_send_kernel(own, got, *outs):
    for k, out in enumerate(outs):
        out[...] = (own[k] + got[k].astype(F32)).astype(out.dtype)


def line_sends(own, got):
    shape = own.shape[1:]
    return call(line_send_kernel, [(shape, F32)] + [(shape, BF16)] * 3, [own, got])


def line_kernel(where, *refs):
    zl = where[2]
    outs, sums = refs[8:12], refs[12]
    for plane in range(2):
        kept, one, two, three = refs[plane * 4 : plane * 4 + 4]
        sums[plane] = (
            kept[...] + one[...].astype(F32) + two[...].astype(F32) + three[...].astype(F32)
        )
    for k, out in enumerate(outs):
        az = lax.rem(zl + k, 4)
        out[...] = sums[lax.div(az, 2), lax.rem(az, 2)].astype(out.dtype)


def line_sums(where, lines):
    block, width = lines[0].shape[1:]
    return call(
        line_kernel,
        [((block, width), F32)] + [((block, width), BF16)] * 3,
        lines,
        scratch=[pltpu.VMEM((2, 2, block, width), F32)],
        where=where,
    )


CHUNK = 384


def outer(lefts, rights, columns_total, emit):
    dims = (((0,), (0,)), ((), ()))

    @pl.loop(0, columns_total // CHUNK)
    def _(i):
        columns = pl.ds(pl.multiple_of(i * CHUNK, CHUNK), CHUNK)
        total = sum(
            lax.dot_general(left(columns), right(), dims, preferred_element_type=F32)
            for left, right in zip(lefts, rights)
        )
        emit(i, columns, total)


def store_out(out, stage, sem, factor):
    def send(i):
        rows = pl.ds(pl.multiple_of(i * CHUNK, CHUNK), CHUNK)
        return pltpu.make_async_copy(stage.at[i], out.at[rows], sem.at[i])

    def emit(i, total):
        stage[i] = (total * factor).astype(BF16)
        send(i).start()

    def finish():
        for i in range(out.shape[0] // CHUNK):
            send(i).wait()

    return emit, finish


def stage_scratch(rows, width):
    return [
        pltpu.VMEM((rows // CHUNK, CHUNK, width), BF16),
        pltpu.SemaphoreType.DMA((rows // CHUNK,)),
    ]


def second_kernel(plane, factor, where, *refs):
    pieces, (own, other), refs = refs[:2], refs[2:4], refs[4:]
    rows = pieces[0].shape[1] // 2
    width = own.shape[-1]
    act = refs[2] if plane else refs[1]
    y = where[1]
    for high, piece in enumerate(pieces):

        @pl.loop(0, 4)
        def _(n):
            low, core = lax.div(n, 2), lax.rem(n, 2)
            ay = lax.bitwise_xor(y, high * 2 + low)
            block = core * 4 + lax.rem(ay + 4 - y, 4)
            values = piece[low, pl.ds(core * rows, rows)].astype(F32)
            act[pl.ds(block * rows, rows)] = gelu_value(values).astype(BF16)

    half = 4 * rows
    lefts = [lambda cols, n=n: act[n * half : (n + 1) * half, cols] for n in range(2)]
    tokens = lax.rem(where[0] + plane, 2)
    rights = [lambda h=h: h[tokens].reshape(-1, width) for h in (own, other)]
    if plane:
        so_far, out, _, stage, sem = refs
        emit, finish = store_out(out, stage, sem, factor)
        outer(
            lefts, rights, act.shape[1], lambda i, cols, t: emit(i, t + so_far[cols])
        )
        finish()
    else:
        total = refs[0]

        def keep(i, cols, value):
            total[cols] = value

        outer(lefts, rights, act.shape[1], keep)


def second_product(where, near, far, halves, factor):
    rows, width = near[0].shape[1:]
    out_width = halves[0].shape[-1]
    flops = 8 * rows * width * out_width
    act = pltpu.VMEM((4 * rows, width), BF16)
    (total,) = call(
        lambda *refs: second_kernel(0, factor, *refs),
        [((width, out_width), F32)],
        [*near, *halves],
        scratch=[act],
        where=where,
        flops=flops,
    )
    return call(
        lambda *refs: second_kernel(1, factor, *refs),
        [((width, out_width), BF16)],
        [*far, *halves, total],
        scratch=[act, *stage_scratch(width, out_width)],
        where=where,
        flops=flops,
        hbm_out=True,
    )[0]


def first_kernel(factor, *refs):
    pieces, (own, other, out, right, stage, sem) = refs[:8], refs[8:]
    rows = pieces[0].shape[0] // 2
    half = 8 * rows
    for i, piece in enumerate(pieces):

        @pl.loop(0, 2)
        def _(core):
            right[pl.ds((core * 8 + i) * rows, rows)] = piece[pl.ds(core * rows, rows)]

    lefts = [
        lambda cols, h=h: h[:, :, :, :, cols].reshape(-1, CHUNK) for h in (own, other)
    ]
    rights = [lambda n=n: right[n * half : (n + 1) * half] for n in range(2)]
    emit, finish = store_out(out, stage, sem, factor)
    outer(lefts, rights, out.shape[0], lambda i, cols, t: emit(i, t))
    finish()


def first_product(pieces, halves, factor):
    rows, width = pieces[0].shape
    out_rows = halves[0].shape[-1]
    return call(
        lambda *refs: first_kernel(factor, *refs),
        [((out_rows, width), BF16)],
        [*pieces, *halves],
        scratch=[pltpu.VMEM((8 * rows, width), BF16), *stage_scratch(out_rows, width)],
        flops=16 * rows * width * out_rows,
        hbm_out=True,
    )[0]


def compute(inputs, out_grad, preact, first_weight, second_weight):
    where = jnp.stack(
        [lax.axis_index(a) for a in ("zh", "y", "zl", "x", "c")]
    ).astype(jnp.int32)
    c = where[4]
    token_rows, width = preact.shape
    block = token_rows // 4
    factor = 1.0 / math.sqrt(8 * token_rows)

    split = preact.reshape(2, 2, block, width)
    preact = jnp.stack(
        [
            jnp.where(c == 0, split[:, 0], split[:, 1]),
            jnp.where(c == 0, split[:, 1], split[:, 0]),
        ]
    ).reshape(token_rows, width)

    grad_half = core_gather(where, out_grad)
    grad_other = swap(grad_half, "c")

    pre_near = jnp.stack([preact, flip(preact, "y", 1)])
    pre = [pre_near, flip(pre_near, "y", 2)]
    pre_far = swap(pre_near, "zh")
    pre += [pre_far, flip(pre_far, "y", 2)]

    part, lead = own_act(grad_half, second_weight)

    def plane_sum(far):
        keep, *sends = other_act(far, grad_other, second_weight, part, lead)
        got = []
        for k, value in zip((1, 2, 3), sends):
            got.append(shift(value, "y", k))
        return row_sum(keep, got)

    sums = [plane_sum(0), plane_sum(1)]

    def exchange(plane):
        total, send = sums[plane]
        return total, swap(send, "zh")

    first = hidden(0, where, *exchange(0), preact, pre_far)
    second = hidden(1, where, *exchange(1), preact, pre_far)
    near, far = spread(first), spread(second)

    def plane_inputs(pieces):
        away, keep = token_products(where, pieces, first_weight)
        got = swap(away, "c")
        keep, *sends = line_sends(keep, got)
        return [keep] + [shift(s, "x", k) for k, s in zip((1, 2, 3), sends)]

    lines = plane_inputs(near) + plane_inputs(far)
    grad_inputs, *sends = line_sums(where, lines)
    got = [shift(s, "zl", k) for k, s in zip((1, 2, 3), sends)]
    grad_inputs = grad_inputs + sum(g.astype(F32) for g in got)

    input_half = core_gather(where, inputs)
    halves = (input_half, swap(input_half, "c"))
    grad_first = first_product(near + far, halves, factor)
    grad_second = second_product(
        where, pre[:2], pre[2:], (grad_half, grad_other), factor
    )
    return (grad_inputs, grad_first, grad_second)


def solution(mesh):
    fine = Mesh(mesh.devices.reshape(2, 4, 4, 4, 2), ("zh", "y", "zl", "x", "c"))
    row, col = ("zh", "y"), ("zl", "x", "c")
    return jax.shard_map(
        compute,
        mesh=fine,
        in_specs=(P(col, row), P(col, row), P(row, col), P(row, col), P(col, row)),
        out_specs=(P(col, row), P(row, col), P(col, row)),
        check_vma=False,
    )
```
